512 devices in a mesh: tm: 16 (over z_hi, y), lat: 32 (over x, z_lo, core).
Axes of the slice: x: 4, y: 4, z: 16 (z_hi: 4, z_lo: 4; z = z_hi * 4 + z_lo), core: 2. Of those that a mesh axis runs over, the one named last changes fastest.
Arguments:
- cotangent: float32 [64, 512, 2048], P('tm', 'lat'), may hold values from -6 to 6
- iterates: float32 [3, 64, 512, 2048], P(None, 'tm', 'lat'), may hold values from -6 to 6
- range_field: float32 [512, 2048], P('lat', 'tm'), may hold values from 0.05 to 1
Outputs:
- noise_cotangent: float32 [64, 512, 2048], P('tm', 'lat')
- range_gradient: float32 [512, 2048], P('lat', 'tm')
The draws below stay inside these ranges and needn't reach their ends.
All inputs are finite; a program needn't handle non-finite values.
Results may differ from the reference program's by a relative error of at most 0.0001.
Values sent between devices are 32-bit elements; how exact they have to be, the bound alone decides.
A program may use at most 64 MiB of HBM per device.

```python
import math
import jax
import jax.numpy as jnp

NX = 2048
STEPS = 4
TIMES = 64
NY = 512


def steps_of(key, dims, cuts, low, high):
    factor_of = 1.0
    for axis_at, blocks in cuts:
        draws = jax.random.uniform(jax.random.fold_in(jax.random.fold_in(key, 6), axis_at), (blocks,), jnp.float32, low / len(cuts), high / len(cuts))
        factor_of = factor_of * jnp.repeat(jnp.exp(draws), dims[axis_at] // blocks).reshape((-1,) + (1,) * (len(dims) - 1 - axis_at))
    return factor_of


def scatter_about(key, shape, spread, most, shards=(), kind=jnp.bfloat16):
    array = jax.random.normal(key, shape, jnp.float32) * spread
    if len(shards) > 0:
        array = steps_of(key, shape, shards, -0.22, 0.18) * array
    return jnp.clip(array, min=-most, max=most).astype(kind)


def setup_inputs(seed: int = 0) -> dict:
    arg_keys = jax.random.split(jax.random.key(seed), 4)
    cotangent = scatter_about(arg_keys[0], (TIMES, NY, NX), 1.0, 6.0, ((0, 16), (1, 32)), jnp.float32)
    iterates = scatter_about(arg_keys[1], (STEPS - 1, TIMES, NY, NX), 1.0, 6.0, ((1, 16), (2, 32)), jnp.float32)
    range_field = jnp.clip(jnp.exp(math.log(1.0) - 2.9957323 * jax.random.uniform(arg_keys[2], (NY, NX), jnp.float32) ** steps_of(arg_keys[2], (NY, NX), ((0, 32), (1, 16)), -0.2, 0.2)), 0.05, 1.0)
    return {"cotangent": cotangent, "iterates": iterates, "range_field": range_field}


def step_weights():
    centre_value = 6.525
    spread_value = 6.475
    root_order = (3, 0, 2, 1)
    return [1.0 / (centre_value + spread_value * math.cos(math.pi * (2 * section + 1) / 8.0)) for section in root_order]


def operate(field, coefficient):
    padded = jnp.pad(field, ((1, 1), (1, 1), (0, 0)))
    latitude = padded[1:-1, 2:, :] + padded[1:-1, :-2, :]
    longitude = jnp.roll(field, 1, 2) + jnp.roll(field, -1, 2)
    temporal = padded[2:, 1:-1, :] + padded[:-2, 1:-1, :]
    return (coefficient[None, :, :] + 6.0) * field - latitude - longitude - temporal


def reference(cotangent, iterates, range_field):
    weights = step_weights()
    adjoint = cotangent
    noise_cot = weights[3] * cotangent
    gradient = jnp.zeros(range_field.shape, jnp.float32)
    for section in (3, 2, 1):
        gradient = gradient - weights[section] * jnp.sum(adjoint * iterates[section - 1], axis=0)
        adjoint = adjoint - weights[section] * operate(adjoint, range_field)
        noise_cot = noise_cot + weights[section - 1] * adjoint
    return noise_cot, gradient
```

```python
import functools
import math

import jax
import jax.numpy as jnp
from jax import lax
from jax.experimental import pallas as pl
from jax.experimental.pallas import tpu as pltpu
from jax.sharding import PartitionSpec as P

MESH = pl.DeviceIdType.MESH
SEG = 16
OWN = 16
PAD = 3
ROWS = OWN + 2 * PAD
OWN_T = 4
SLICES = OWN_T + 2 * PAD
SHARE = ((0, 5), (5, 4), (9, 4), (13, 3))


def step_weights():
    centre_value = 6.525
    spread_value = 6.475
    root_order = (3, 0, 2, 1)
    return [
        1.0 / (centre_value + spread_value * math.cos(math.pi * (2 * section + 1) / 8.0))
        for section in root_order
    ]


def at_row(row):
    return (row + PAD) * SEG


class Sems:
    def __init__(self):
        self.names = {}

    def __call__(self, *key):
        return self.names.setdefault(key, len(self.names))


def kernel(
    lats, sem_of, cot, its, rng, noise, grad,
    cin, xin, field4, field3, field2, coef, gathered, relay, part, part_in, total, total_in,
    send, recv, local,
):
    weights = step_weights()
    tm = lax.axis_index("tm")
    lat = lax.axis_index("lat")
    z, y = lax.div(tm, 4), lax.rem(tm, 4)
    z_next, z_prev = lax.rem(z + 1, 4), lax.rem(z + 3, 4)
    lat_next, lat_prev = lax.rem(lat + 1, lats), lax.rem(lat + lats - 1, lats)

    def dev(zz, yy, ll=None):
        return (zz * 4 + yy, lat if ll is None else ll)

    barrier = pltpu.get_barrier_semaphore()

    def greet(device):
        pl.semaphore_signal(barrier, inc=1, device_id=device, device_id_type=MESH)

    for other in (1, 2, 3):
        greet(dev(z, lax.rem(y + other, 4)))
    greet(dev(z, y, lat_next))
    greet(dev(z, y, lat_prev))
    greet(dev(z_next, y))
    greet(dev(z_prev, y))

    @pl.when(y == 0)
    def _():
        for plane in (1, 2, 3):
            greet(dev(z_prev, plane))

    @pl.when(y == 3)
    def _():
        for plane in (0, 1, 2):
            greet(dev(z_next, plane))

    loads = [pltpu.make_async_copy(cot.at[t], cin.at[t], local.at[t]) for t in range(OWN_T)]
    for t in (3, 0, 2, 1):
        loads[t].start()
    load_range = pltpu.make_async_copy(rng, gathered.at[y * 4 + z], local.at[4])
    load_range.start()
    load_its = pltpu.make_async_copy(its, xin, local.at[5])
    load_its.start()

    def zero(ref, t, row, rows):
        ref[t + PAD, pl.ds(at_row(row), rows * SEG), :] = jnp.zeros((rows * SEG, 128), jnp.float32)

    @pl.when(lat == 0)
    def _():
        for ref in (field4, field3, field2):
            for t in range(-PAD, OWN_T + PAD):
                zero(ref, t, -PAD, PAD)

    @pl.when(lat == lats - 1)
    def _():
        for ref in (field4, field3, field2):
            for t in range(-PAD, OWN_T + PAD):
                zero(ref, t, OWN, PAD)

    @pl.when(tm == 0)
    def _():
        for ref in (field4, field3, field2):
            for t in range(-PAD, 0):
                zero(ref, t, -PAD, ROWS)

    @pl.when(tm == 15)
    def _():
        for ref in (field4, field3, field2):
            for t in range(OWN_T, OWN_T + PAD):
                zero(ref, t, -PAD, ROWS)

    for t in (3, 0, 2, 1):
        loads[t].wait()
        for group in range(2):
            for j in range(16):
                field4[t + PAD, pl.ds(at_row(group * 8) + j, 8, stride=SEG), :] = cin[
                    t, group * 8 : group * 8 + 8, j * 128 : j * 128 + 128
                ]
    load_range.wait()

    ends = jnp.logical_or(y == 0, y == 3)

    @pl.when(ends)
    def _():
        pl.semaphore_wait(barrier, 8)

    @pl.when(jnp.logical_not(ends))
    def _():
        pl.semaphore_wait(barrier, 9)

    sends = []

    def copy(key, src, dst, device):
        index = sem_of(*key)
        return pltpu.make_async_remote_copy(
            src_ref=src, dst_ref=dst, send_sem=send.at[index], recv_sem=recv.at[index],
            device_id=device, device_id_type=MESH,
        )

    def start(condition, made):
        if condition is None:
            made.start()
        else:
            pl.when(condition)(made.start)
        sends.append((condition, made))

    def arrived(condition, made):
        if condition is None:
            made.wait_recv()
        else:
            pl.when(condition)(made.wait_recv)

    def block(ref, t, row, rows):
        return ref.at[t + PAD, pl.ds(at_row(row), rows * SEG), :]

    has_lat_prev, has_lat_next = lat > 0, lat < lats - 1

    def range_z(way):
        origin = gathered.at[y * 4 + z]
        return copy(("rz", way), origin, origin, dev(z_next if way > 0 else z_prev, y))

    def range_z_second():
        slot = gathered.at[y * 4 + z_prev]
        return copy(("rz2",), slot, slot, dev(z_next, y))

    def range_y(other):
        slots = gathered.at[pl.ds(y * 4, 4)]
        return copy(("ry", other), slots, slots, dev(z, lax.rem(y + other, 4)))

    def range_lat(way):
        if way > 0:
            src, dst = coef.at[pl.ds(at_row(OWN - 2), 2 * SEG)], coef.at[pl.ds(at_row(-2), 2 * SEG)]
        else:
            src, dst = coef.at[pl.ds(at_row(0), 2 * SEG)], coef.at[pl.ds(at_row(OWN), 2 * SEG)]
        return copy(("rl", way), src, dst, dev(z, y, lat_next if way > 0 else lat_prev))

    def lat_halo(way):
        own = pl.ds(PAD, OWN_T)
        if way > 0:
            src, dst = OWN - PAD, -PAD
        else:
            src, dst = 0, OWN
        return copy(
            ("lat", way),
            field4.at[own, pl.ds(at_row(src), PAD * SEG), :],
            field4.at[own, pl.ds(at_row(dst), PAD * SEG), :],
            dev(z, y, lat_next if way > 0 else lat_prev),
        )

    def slices(way, depth):
        return (OWN_T - depth, -depth) if way > 0 else (depth - 1, OWN_T - 1 + depth)

    def beside(way, depth):
        src, dst = slices(way, depth)
        return copy(
            ("t", way, depth), block(field4, src, 0, OWN), block(field4, dst, 0, OWN), dev(z, y + way)
        )

    def across(way):
        return dev(z_next, 0) if way > 0 else dev(z_prev, 3)

    def to_relay(way, depth, plane):
        first, rows = SHARE[plane]
        src, _ = slices(way, depth)
        return copy(
            ("a", way, depth),
            block(field4, src, first, rows),
            relay.at[(way + 1) // 2, depth - 1, pl.ds(0, rows * SEG)],
            dev(z, plane if way > 0 else 3 - plane),
        )

    def to_relay_send(way, depth, plane):
        first, rows = SHARE[plane]
        src, _ = slices(way, depth)
        return pltpu.make_async_remote_copy(
            src_ref=block(field4, src, first, rows),
            dst_ref=relay.at[(way + 1) // 2, depth - 1, pl.ds(0, rows * SEG)],
            send_sem=send.at[sem_of("as", way, depth, plane)],
            recv_sem=recv.at[sem_of("a", way, depth)],
            device_id=dev(z, plane if way > 0 else 3 - plane),
            device_id_type=MESH,
        )

    def from_relay(way, depth, plane):
        first, rows = SHARE[plane]
        src, dst = slices(way, depth)
        source = (
            block(field4, src, first, rows)
            if plane == 3
            else relay.at[(way + 1) // 2, depth - 1, pl.ds(0, rows * SEG)]
        )
        return copy(("b", way, depth, plane), source, block(field4, dst, first, rows), across(way))

    corners = ((1, -2, 2), (1, OWN, 2), (2, -1, 1), (2, OWN, 1))

    def corner(way, number, crossing):
        depth, row, rows = corners[number]
        src, dst = slices(way, depth)
        return copy(
            ("c", way, number),
            block(field4, src, row, rows),
            block(field4, dst, row, rows),
            across(way) if crossing else dev(z, y + way),
        )

    def is_source(way):
        return jnp.logical_and(y == 3, z < 3) if way > 0 else jnp.logical_and(y == 0, z > 0)

    def is_target(way):
        return jnp.logical_and(y == 0, z > 0) if way > 0 else jnp.logical_and(y == 3, z < 3)

    def is_relay(way, plane):
        return (
            jnp.logical_and(y == plane, z < 3) if way > 0 else jnp.logical_and(y == 3 - plane, z > 0)
        )

    def beside_out(way):
        return y < 3 if way > 0 else y > 0

    def beside_in(way):
        return y > 0 if way > 0 else y < 3

    def lat_edge(row):
        return has_lat_prev if row < 0 else has_lat_next

    def send_slices(depth):
        for way in (1, -1):
            for plane in (0, 1, 2):
                start(is_source(way), to_relay_send(way, depth, plane))
            start(is_source(way), from_relay(way, depth, 3))
            start(beside_out(way), beside(way, depth))

    def forward(depth):
        for way in (1, -1):
            for plane in (0, 1, 2):
                arrived(is_relay(way, plane), to_relay(way, depth, plane))
                start(is_relay(way, plane), from_relay(way, depth, plane))

    def wait_slices(depth):
        for way in (1, -1):
            arrived(beside_in(way), beside(way, depth))
            for plane in range(4):
                arrived(is_target(way), from_relay(way, depth, plane))

    def send_corners():
        for way in (1, -1):
            for number in range(4):
                inside = lat_edge(corners[number][1])
                start(jnp.logical_and(beside_out(way), inside), corner(way, number, False))
                start(jnp.logical_and(is_source(way), inside), corner(way, number, True))

    def wait_corners(depth):
        for way in (1, -1):
            for number in range(4):
                if corners[number][0] == depth:
                    inside = lat_edge(corners[number][1])
                    coming = jnp.logical_or(beside_in(way), is_target(way))
                    arrived(jnp.logical_and(coming, inside), corner(way, number, False))

    lane = lax.broadcasted_iota(jnp.int32, (SEG, 128), 1)

    def row_of(src, t, base):
        return src[t, pl.ds(base, SEG), :]

    def stepped(src, t, base, weight):
        cells = row_of(src, t, base)
        around = (
            row_of(src, t, base - SEG)
            + row_of(src, t, base + SEG)
            + row_of(src, t - 1, base)
            + row_of(src, t + 1, base)
        )
        west = pltpu.roll(cells, 1, 1)
        west = jnp.where(lane == 0, pltpu.roll(west, 1, 0), west)
        east = pltpu.roll(cells, 127, 1)
        east = jnp.where(lane == 127, pltpu.roll(east, SEG - 1, 0), east)
        applied = coef[pl.ds(base, SEG), :] * cells - (around + (west + east))
        return cells - weight * applied

    UNROLL = 8

    def step(dst, src, t_first, t_count, t_stride, weight, outer):
        pieces = OWN // UNROLL

        def piece(i, carry):
            t = t_first + PAD + lax.div(i, pieces) * t_stride
            base = pl.multiple_of(at_row(0) + lax.rem(i, pieces) * (UNROLL * SEG), SEG)
            for row in range(UNROLL):
                here = base + row * SEG
                dst[t, pl.ds(here, SEG), :] = stepped(src, t, here, weight)
            return carry

        lax.fori_loop(0, t_count * pieces, piece, 0)

        def beyond(first, rows):
            def one(i, carry):
                t = t_first + PAD + i * t_stride
                for row in range(first, first + rows):
                    dst[t, pl.ds(at_row(row), SEG), :] = stepped(src, t, at_row(row), weight)
                return carry

            lax.fori_loop(0, t_count, one, 0)

        if outer:
            pl.when(has_lat_prev)(lambda: beyond(-outer, outer))
            pl.when(has_lat_next)(lambda: beyond(OWN, outer))

    def products(terms, first):
        def column(j, carry):
            for group in range(2):
                value = None
                for ref, k, t in terms:
                    adj = ref[t + PAD, pl.ds(at_row(group * 8) + j, 8, stride=SEG), :]
                    x = xin[k - 1, t, group * 8 : group * 8 + 8, pl.ds(pl.multiple_of(j * 128, 128), 128)]
                    term = (-weights[k]) * (adj * x)
                    value = term if value is None else value + term
                slot = lax.rem(j, 4) * 4 + lax.div(j, 4)
                rows = slice(group * 8, group * 8 + 8)
                part[slot, rows, :] = value if first else part[slot, rows, :] + value
            return carry

        lax.fori_loop(0, 16, column, 0)

    start(None, range_z(1))
    start(None, range_z(-1))
    start(has_lat_next, lat_halo(1))
    start(has_lat_prev, lat_halo(-1))
    send_slices(1)
    send_slices(2)
    forward(1)
    arrived(has_lat_prev, lat_halo(1))
    arrived(has_lat_next, lat_halo(-1))
    send_corners()
    forward(2)
    send_slices(3)
    arrived(None, range_z(1))
    start(None, range_z_second())
    load_its.wait()
    products([(field4, 3, t) for t in range(OWN_T)], True)
    arrived(None, range_z(-1))
    forward(3)
    arrived(None, range_z_second())
    for other in (1, 2, 3):
        start(None, range_y(other))
    for other in (1, 2, 3):
        arrived(None, range_y(other))
    for j in range(16):
        slot = (j % 4) * 4 + j // 4
        for group in range(2):
            coef[pl.ds(at_row(group * 8) + j, 8, stride=SEG), :] = (
                gathered[slot, group * 8 : group * 8 + 8, :] + 6.0
            )
    start(has_lat_next, range_lat(1))
    start(has_lat_prev, range_lat(-1))
    arrived(has_lat_prev, range_lat(1))
    arrived(has_lat_next, range_lat(-1))

    step(field3, field4, 1, 2, 1, weights[3], 2)
    wait_slices(1)
    wait_corners(1)
    step(field3, field4, 0, 2, 3, weights[3], 2)
    step(field2, field3, 1, 2, 1, weights[2], 1)
    products([(field3, 2, t) for t in range(OWN_T)] + [(field2, 1, 1), (field2, 1, 2)], False)
    wait_slices(2)
    wait_corners(2)
    pl.when(tm > 0)(lambda: step(field3, field4, -1, 1, 1, weights[3], 1))
    pl.when(tm < 15)(lambda: step(field3, field4, OWN_T, 1, 1, weights[3], 1))
    step(field2, field3, 0, 2, 3, weights[2], 1)
    products([(field2, 1, 0), (field2, 1, 3)], False)

    def sum_y(other):
        target = lax.rem(y + other, 4)
        return copy(("sy", other), part.at[pl.ds(target * 4, 4)], part_in.at[other - 1], dev(z, target))

    def sum_z(number):
        which = (lax.rem(z + 2, 4), z_prev, z_next)[number]
        return copy(("sz", number), total.at[which], total_in.at[number], dev(z_prev if number == 1 else z_next, y))

    def finish(t_first, t_count, t_stride):
        pieces = OWN // UNROLL

        def piece(i, carry):
            t = t_first + PAD + lax.div(i, pieces) * t_stride
            base = pl.multiple_of(at_row(0) + lax.rem(i, pieces) * (UNROLL * SEG), SEG)
            for row in range(UNROLL):
                here = base + row * SEG
                last = stepped(field2, t, here, weights[1])
                noise[t - PAD, pl.ds(here - at_row(0), SEG), :] = (
                    weights[3] * row_of(field4, t, here)
                    + weights[2] * row_of(field3, t, here)
                    + weights[1] * row_of(field2, t, here)
                    + weights[0] * last
                )
            return carry

        lax.fori_loop(0, t_count * pieces, piece, 0)

    for other in (1, 2, 3):
        start(None, sum_y(other))
    finish(1, 2, 1)
    for other in (1, 2, 3):
        arrived(None, sum_y(other))
    for zz in range(4):
        total[zz] = part[y * 4 + zz] + part_in[0, zz] + part_in[1, zz] + part_in[2, zz]
    start(None, sum_z(0))
    start(None, sum_z(1))
    wait_slices(3)
    pl.when(tm > 0)(lambda: step(field3, field4, -2, 1, 1, weights[3], 0))
    pl.when(tm < 15)(lambda: step(field3, field4, OWN_T + 1, 1, 1, weights[3], 0))
    pl.when(tm > 0)(lambda: step(field2, field3, -1, 1, 1, weights[2], 0))
    pl.when(tm < 15)(lambda: step(field2, field3, OWN_T, 1, 1, weights[2], 0))
    arrived(None, sum_z(0))
    total[z_next] = total[z_next] + total_in[0]
    start(None, sum_z(2))
    finish(0, 2, 3)
    arrived(None, sum_z(1))
    arrived(None, sum_z(2))
    grad[...] = total[z] + total_in[1] + total_in[2]

    for condition, made in sends:
        if condition is None:
            made.wait_send()
        else:
            pl.when(condition)(made.wait_send)


def place(noise_rows, grad_in, noise, grad):
    def columns(i, carry):
        t, j = lax.div(i, 16), lax.rem(i, 16)
        for group in range(2):
            noise[t, group * 8 : group * 8 + 8, pl.ds(pl.multiple_of(j * 128, 128), 128)] = noise_rows[
                t, pl.ds(group * 8 * SEG + j, 8, stride=SEG), :
            ]
        return carry

    lax.fori_loop(0, OWN_T * 16, columns, 0)
    grad[...] = grad_in[...]


def vmem(*shape):
    return pltpu.VMEM(shape, jnp.float32)


def body(lats, cotangent, iterates, range_field):
    anywhere = pl.BlockSpec(memory_space=pl.ANY)
    inside = pl.BlockSpec(memory_space=pltpu.VMEM)
    count = 128
    noise_rows, grad = pl.pallas_call(
        functools.partial(kernel, lats, Sems()),
        out_shape=(
            jax.ShapeDtypeStruct((OWN_T, OWN * SEG, 128), jnp.float32),
            jax.ShapeDtypeStruct(range_field.shape, jnp.float32),
        ),
        in_specs=[anywhere] * 3,
        out_specs=(inside, inside),
        scratch_shapes=[
            vmem(OWN_T, OWN, 2048),
            vmem(3, OWN_T, OWN, 2048),
            vmem(SLICES, ROWS * SEG, 128),
            vmem(SLICES, ROWS * SEG, 128),
            vmem(SLICES, ROWS * SEG, 128),
            vmem(ROWS * SEG, 128),
            vmem(16, OWN, 128),
            vmem(2, PAD, 5 * SEG, 128),
            vmem(16, OWN, 128),
            vmem(3, 4, OWN, 128),
            vmem(4, OWN, 128),
            vmem(3, OWN, 128),
            pltpu.SemaphoreType.DMA((count,)),
            pltpu.SemaphoreType.DMA((count,)),
            pltpu.SemaphoreType.DMA((6,)),
        ],
        compiler_params=pltpu.CompilerParams(
            collective_id=0, has_side_effects=True, vmem_limit_bytes=32 << 20
        ),
        name="adjoint",
    )(cotangent, iterates, range_field)
    return pl.pallas_call(
        place,
        out_shape=(
            jax.ShapeDtypeStruct(cotangent.shape, jnp.float32),
            jax.ShapeDtypeStruct(range_field.shape, jnp.float32),
        ),
        in_specs=[inside, inside],
        out_specs=(inside, inside),
        name="place",
    )(noise_rows, grad)


def solution(mesh):
    placed = (P("tm", "lat", None), P(None, "tm", "lat", None), P("lat", "tm"))
    return jax.shard_map(
        functools.partial(body, mesh.shape["lat"]),
        mesh=mesh,
        in_specs=placed,
        out_specs=(P("tm", "lat", None), P("lat", "tm")),
        check_vma=False,
    )
```

```python
import functools
import math

import jax
import jax.numpy as jnp
from jax import lax
from jax.experimental import pallas as pl
from jax.experimental.pallas import tpu as pltpu
from jax.sharding import PartitionSpec as P

MESH = pl.DeviceIdType.MESH
SEG = 16
OWN = 16
PAD = 3
ROWS = OWN + 2 * PAD
OWN_T = 4
SLICES = OWN_T + 2 * PAD
SHARE = ((0, 5), (5, 4), (9, 4), (13, 3))


def step_weights():
    centre_value = 6.525
    spread_value = 6.475
    root_order = (3, 0, 2, 1)
    return [
        1.0 / (centre_value + spread_value * math.cos(math.pi * (2 * section + 1) / 8.0))
        for section in root_order
    ]


def at_row(row):
    return (row + PAD) * SEG


class Sems:
    def __init__(self):
        self.names = {}

    def __call__(self, *key):
        return self.names.setdefault(key, len(self.names))


def kernel(
    lats, sem_of, cot, its, rng, noise, grad,
    cin, xin, field4, field3, field2, rows_out, coef, gathered, relay, part, part_in, total, total_in,
    send, recv, local,
):
    weights = step_weights()
    tm = lax.axis_index("tm")
    lat = lax.axis_index("lat")
    z, y = lax.div(tm, 4), lax.rem(tm, 4)
    z_next, z_prev = lax.rem(z + 1, 4), lax.rem(z + 3, 4)
    lat_next, lat_prev = lax.rem(lat + 1, lats), lax.rem(lat + lats - 1, lats)

    def dev(zz, yy, ll=None):
        return (zz * 4 + yy, lat if ll is None else ll)

    barrier = pltpu.get_barrier_semaphore()

    def greet(device):
        pl.semaphore_signal(barrier, inc=1, device_id=device, device_id_type=MESH)

    greet(dev(z_next, y))
    greet(dev(z_prev, y))

    @pl.when(y == 0)
    def _():
        for plane in (1, 2, 3):
            greet(dev(z_prev, plane))

    @pl.when(y == 3)
    def _():
        for plane in (0, 1, 2):
            greet(dev(z_next, plane))

    greet(dev(z, y, lat_next))
    greet(dev(z, y, lat_prev))
    for other in (1, 2, 3):
        greet(dev(z, lax.rem(y + other, 4)))

    loads = [pltpu.make_async_copy(cot.at[t], cin.at[t], local.at[t]) for t in range(OWN_T)]
    for t in (3, 0, 2, 1):
        loads[t].start()
    load_range = pltpu.make_async_copy(rng, gathered.at[y * 4 + z], local.at[4])
    load_range.start()
    load_its = pltpu.make_async_copy(its, xin, local.at[5])
    load_its.start()

    def zero(ref, t, row, rows):
        ref[t + PAD, pl.ds(at_row(row), rows * SEG), :] = jnp.zeros((rows * SEG, 128), jnp.float32)

    @pl.when(lat == 0)
    def _():
        for ref in (field4, field3, field2):
            for t in range(-PAD, OWN_T + PAD):
                zero(ref, t, -PAD, PAD)

    @pl.when(lat == lats - 1)
    def _():
        for ref in (field4, field3, field2):
            for t in range(-PAD, OWN_T + PAD):
                zero(ref, t, OWN, PAD)

    @pl.when(tm == 0)
    def _():
        for ref in (field4, field3, field2):
            for t in range(-PAD, 0):
                zero(ref, t, -PAD, ROWS)

    @pl.when(tm == 15)
    def _():
        for ref in (field4, field3, field2):
            for t in range(OWN_T, OWN_T + PAD):
                zero(ref, t, -PAD, ROWS)

    for t in (3, 0, 2, 1):
        loads[t].wait()
        for group in range(2):
            for j in range(16):
                field4[t + PAD, pl.ds(at_row(group * 8) + j, 8, stride=SEG), :] = cin[
                    t, group * 8 : group * 8 + 8, j * 128 : j * 128 + 128
                ]
    load_range.wait()

    ends = jnp.logical_or(y == 0, y == 3)

    @pl.when(ends)
    def _():
        pl.semaphore_wait(barrier, 8)

    @pl.when(jnp.logical_not(ends))
    def _():
        pl.semaphore_wait(barrier, 9)

    sends = []

    def copy(key, src, dst, device):
        index = sem_of(*key)
        return pltpu.make_async_remote_copy(
            src_ref=src, dst_ref=dst, send_sem=send.at[index], recv_sem=recv.at[index],
            device_id=device, device_id_type=MESH,
        )

    def start(condition, *made):
        if condition is None:
            for one in made:
                one.start()
        else:

            @pl.when(condition)
            def _():
                for one in made:
                    one.start()

        sends.append((condition, made))

    def arrived(condition, *made):
        if condition is None:
            for one in made:
                one.wait_recv()
        else:

            @pl.when(condition)
            def _():
                for one in made:
                    one.wait_recv()

    def sent():
        for condition, made in sends:
            if condition is None:
                for one in made:
                    one.wait_send()
            else:

                @pl.when(condition)
                def _():
                    for one in made:
                        one.wait_send()

        sends.clear()

    def block(ref, t, row, rows):
        return ref.at[t + PAD, pl.ds(at_row(row), rows * SEG), :]

    has_lat_prev, has_lat_next = lat > 0, lat < lats - 1

    def range_z(way):
        origin = gathered.at[y * 4 + z]
        return copy(("rz", way), origin, origin, dev(z_next if way > 0 else z_prev, y))

    def range_z_second():
        slot = gathered.at[y * 4 + z_prev]
        return copy(("rz2",), slot, slot, dev(z_next, y))

    def range_y(number, other):
        slot = gathered.at[y * 4 + (z, z_prev, z_next, lax.rem(z + 2, 4))[number]]
        return copy(("ry", number, other), slot, slot, dev(z, lax.rem(y + other, 4)))

    def share_range(number):
        for other in (1, 2, 3):
            start(None, range_y(number, other))

    def range_lat(way):
        if way > 0:
            src, dst = coef.at[pl.ds(at_row(OWN - 2), 2 * SEG)], coef.at[pl.ds(at_row(-2), 2 * SEG)]
        else:
            src, dst = coef.at[pl.ds(at_row(0), 2 * SEG)], coef.at[pl.ds(at_row(OWN), 2 * SEG)]
        return copy(("rl", way), src, dst, dev(z, y, lat_next if way > 0 else lat_prev))

    def lat_halo(way):
        own = pl.ds(PAD, OWN_T)
        if way > 0:
            src, dst = OWN - PAD, -PAD
        else:
            src, dst = 0, OWN
        return copy(
            ("lat", way),
            field4.at[own, pl.ds(at_row(src), PAD * SEG), :],
            field4.at[own, pl.ds(at_row(dst), PAD * SEG), :],
            dev(z, y, lat_next if way > 0 else lat_prev),
        )

    def slices(way, depth):
        return (OWN_T - depth, -depth) if way > 0 else (depth - 1, OWN_T - 1 + depth)

    def beside(way, depth):
        src, dst = slices(way, depth)
        return copy(
            ("t", way, depth), block(field4, src, 0, OWN), block(field4, dst, 0, OWN), dev(z, y + way)
        )

    def across(way):
        return dev(z_next, 0) if way > 0 else dev(z_prev, 3)

    def to_relay(way, depth, plane):
        first, rows = SHARE[plane]
        src, _ = slices(way, depth)
        return copy(
            ("a", way, depth),
            block(field4, src, first, rows),
            relay.at[(way + 1) // 2, depth - 1, pl.ds(0, rows * SEG)],
            dev(z, plane if way > 0 else 3 - plane),
        )

    def to_relay_send(way, depth, plane):
        first, rows = SHARE[plane]
        src, _ = slices(way, depth)
        return pltpu.make_async_remote_copy(
            src_ref=block(field4, src, first, rows),
            dst_ref=relay.at[(way + 1) // 2, depth - 1, pl.ds(0, rows * SEG)],
            send_sem=send.at[sem_of("as", way, depth, plane)],
            recv_sem=recv.at[sem_of("a", way, depth)],
            device_id=dev(z, plane if way > 0 else 3 - plane),
            device_id_type=MESH,
        )

    def from_relay(way, depth, plane):
        first, rows = SHARE[plane]
        src, dst = slices(way, depth)
        source = (
            block(field4, src, first, rows)
            if plane == 3
            else relay.at[(way + 1) // 2, depth - 1, pl.ds(0, rows * SEG)]
        )
        return copy(("b", way, depth, plane), source, block(field4, dst, first, rows), across(way))

    corners = ((1, -2, 2), (1, OWN, 2), (2, -1, 1), (2, OWN, 1))

    def corner(way, number, crossing):
        depth, row, rows = corners[number]
        src, dst = slices(way, depth)
        return copy(
            ("c", way, number),
            block(field4, src, row, rows),
            block(field4, dst, row, rows),
            across(way) if crossing else dev(z, y + way),
        )

    def is_source(way):
        return jnp.logical_and(y == 3, z < 3) if way > 0 else jnp.logical_and(y == 0, z > 0)

    def is_target(way):
        return jnp.logical_and(y == 0, z > 0) if way > 0 else jnp.logical_and(y == 3, z < 3)

    def is_relay(way, plane):
        return (
            jnp.logical_and(y == plane, z < 3) if way > 0 else jnp.logical_and(y == 3 - plane, z > 0)
        )

    def beside_out(way):
        return y < 3 if way > 0 else y > 0

    def beside_in(way):
        return y > 0 if way > 0 else y < 3

    def lat_edge(row):
        return has_lat_prev if row < 0 else has_lat_next

    def send_slices(depth):
        for way in (1, -1):
            start(
                is_source(way),
                *[to_relay_send(way, depth, plane) for plane in (0, 1, 2)],
                from_relay(way, depth, 3),
            )
            start(beside_out(way), beside(way, depth))

    def forward(depth):
        for way in (1, -1):
            for plane in (0, 1, 2):

                @pl.when(is_relay(way, plane))
                def _():
                    to_relay(way, depth, plane).wait_recv()
                    from_relay(way, depth, plane).start()

                sends.append((is_relay(way, plane), (from_relay(way, depth, plane),)))

    def wait_slices(depth):
        for way in (1, -1):
            arrived(beside_in(way), beside(way, depth))
            arrived(is_target(way), *[from_relay(way, depth, plane) for plane in range(4)])

    def send_corners():
        for way in (1, -1):
            for pair in ((0, 2), (1, 3)):
                inside = lat_edge(corners[pair[0]][1])
                start(
                    jnp.logical_and(beside_out(way), inside),
                    *[corner(way, number, False) for number in pair],
                )
                start(
                    jnp.logical_and(is_source(way), inside),
                    *[corner(way, number, True) for number in pair],
                )

    def wait_corners(depth):
        for way in (1, -1):
            for number in range(4):
                if corners[number][0] == depth:
                    inside = lat_edge(corners[number][1])
                    coming = jnp.logical_or(beside_in(way), is_target(way))
                    arrived(jnp.logical_and(coming, inside), corner(way, number, False))

    lane = lax.broadcasted_iota(jnp.int32, (SEG, 128), 1)

    def row_of(src, t, base):
        return src[t, pl.ds(base, SEG), :]

    def neighbours(src, t, base):
        cells = row_of(src, t, base)
        around = (
            row_of(src, t, base - SEG)
            + row_of(src, t, base + SEG)
            + row_of(src, t - 1, base)
            + row_of(src, t + 1, base)
        )
        west = pltpu.roll(cells, 1, 1)
        west = jnp.where(lane == 0, pltpu.roll(west, 1, 0), west)
        east = pltpu.roll(cells, 127, 1)
        east = jnp.where(lane == 127, pltpu.roll(east, SEG - 1, 0), east)
        return around + (west + east)

    def joined(src, t, base, weight, summed):
        cells = row_of(src, t, base)
        return cells - weight * (coef[pl.ds(base, SEG), :] * cells - summed)

    def stepped(src, t, base, weight):
        return joined(src, t, base, weight, neighbours(src, t, base))

    UNROLL = 8

    def step(dst, src, t_first, t_count, t_stride, weight, outer, how=None):
        def stepped_by(src, t, base, weight):
            if how == "gather":
                return neighbours(src, t, base)
            if how == "join":
                return joined(src, t, base, weight, row_of(dst, t, base))
            return stepped(src, t, base, weight)

        pieces = OWN // UNROLL

        def piece(i, carry):
            t = t_first + PAD + lax.div(i, pieces) * t_stride
            base = pl.multiple_of(at_row(0) + lax.rem(i, pieces) * (UNROLL * SEG), SEG)
            for row in range(UNROLL):
                here = base + row * SEG
                dst[t, pl.ds(here, SEG), :] = stepped_by(src, t, here, weight)
            return carry

        lax.fori_loop(0, t_count * pieces, piece, 0)

        def beyond(first, rows):
            def one(i, carry):
                t = t_first + PAD + i * t_stride
                for row in range(first, first + rows):
                    dst[t, pl.ds(at_row(row), SEG), :] = stepped_by(src, t, at_row(row), weight)
                return carry

            lax.fori_loop(0, t_count, one, 0)

        if outer:
            pl.when(has_lat_prev)(lambda: beyond(-outer, outer))
            pl.when(has_lat_next)(lambda: beyond(OWN, outer))

    def products(terms, first):
        def column(j, carry):
            for group in range(2):
                value = None
                for ref, k, t in terms:
                    adj = ref[t + PAD, pl.ds(at_row(group * 8) + j, 8, stride=SEG), :]
                    x = xin[k - 1, t, group * 8 : group * 8 + 8, pl.ds(pl.multiple_of(j * 128, 128), 128)]
                    term = (-weights[k]) * (adj * x)
                    value = term if value is None else value + term
                slot = lax.rem(j, 4) * 4 + lax.div(j, 4)
                rows = slice(group * 8, group * 8 + 8)
                part[slot, rows, :] = value if first else part[slot, rows, :] + value
            return carry

        lax.fori_loop(0, 16, column, 0)

    start(None, range_z(1))
    start(None, range_z(-1))
    start(has_lat_next, lat_halo(1))
    start(has_lat_prev, lat_halo(-1))
    share_range(0)
    send_slices(1)
    forward(1)
    arrived(None, range_z(1))
    start(None, range_z_second())
    share_range(1)
    arrived(None, range_z(-1))
    share_range(2)
    send_slices(2)
    arrived(has_lat_prev, lat_halo(1))
    arrived(has_lat_next, lat_halo(-1))
    send_corners()
    forward(2)
    load_its.wait()
    products([(field4, 3, t) for t in range(OWN_T)], True)
    arrived(None, range_z_second())
    share_range(3)
    send_slices(3)
    step(field3, field4, 1, 2, 1, weights[3], 2, "gather")
    for number in range(4):
        for other in (1, 2, 3):
            arrived(None, range_y(number, other))
    for j in range(16):
        slot = (j % 4) * 4 + j // 4
        for group in range(2):
            coef[pl.ds(at_row(group * 8) + j, 8, stride=SEG), :] = (
                gathered[slot, group * 8 : group * 8 + 8, :] + 6.0
            )
    start(has_lat_next, range_lat(1))
    start(has_lat_prev, range_lat(-1))
    wait_slices(1)
    wait_corners(1)
    step(field3, field4, 0, 2, 3, weights[3], 2, "gather")
    forward(3)
    arrived(has_lat_prev, range_lat(1))
    arrived(has_lat_next, range_lat(-1))
    step(field3, field4, 0, 4, 1, weights[3], 2, "join")
    step(field2, field3, 1, 2, 1, weights[2], 1)
    products([(field3, 2, t) for t in range(OWN_T)] + [(field2, 1, 1), (field2, 1, 2)], False)
    wait_slices(2)
    wait_corners(2)
    pl.when(tm > 0)(lambda: step(field3, field4, -1, 1, 1, weights[3], 1))
    pl.when(tm < 15)(lambda: step(field3, field4, OWN_T, 1, 1, weights[3], 1))
    step(field2, field3, 0, 2, 3, weights[2], 1)
    products([(field2, 1, 0), (field2, 1, 3)], False)

    def sum_y(other):
        target = lax.rem(y + other, 4)
        return copy(("sy", other), part.at[pl.ds(target * 4, 4)], part_in.at[other - 1], dev(z, target))

    def sum_z(number):
        which = (lax.rem(z + 2, 4), z_prev, z_next)[number]
        return copy(("sz", number), total.at[which], total_in.at[number], dev(z_prev if number == 1 else z_next, y))

    def finish(t_first, t_count, t_stride):
        pieces = OWN // UNROLL

        def piece(i, carry):
            t = t_first + PAD + lax.div(i, pieces) * t_stride
            base = pl.multiple_of(at_row(0) + lax.rem(i, pieces) * (UNROLL * SEG), SEG)
            for row in range(UNROLL):
                here = base + row * SEG
                last = stepped(field2, t, here, weights[1])
                rows_out[t - PAD, pl.ds(here - at_row(0), SEG), :] = (
                    weights[3] * row_of(field4, t, here)
                    + weights[2] * row_of(field3, t, here)
                    + weights[1] * row_of(field2, t, here)
                    + weights[0] * last
                )
            return carry

        lax.fori_loop(0, t_count * pieces, piece, 0)

        def columns(i, carry):
            t = t_first + lax.div(i, 16) * t_stride
            j = lax.rem(i, 16)
            for group in range(2):
                noise[t, group * 8 : group * 8 + 8, pl.ds(pl.multiple_of(j * 128, 128), 128)] = rows_out[
                    t, pl.ds(group * 8 * SEG + j, 8, stride=SEG), :
                ]
            return carry

        lax.fori_loop(0, t_count * 16, columns, 0)

    for other in (1, 2, 3):
        start(None, sum_y(other))
    finish(1, 2, 1)
    for other in (1, 2, 3):
        arrived(None, sum_y(other))
    for zz in range(4):
        total[zz] = part[y * 4 + zz] + part_in[0, zz] + part_in[1, zz] + part_in[2, zz]
    start(None, sum_z(0), sum_z(1))
    wait_slices(3)
    pl.when(tm > 0)(lambda: step(field3, field4, -2, 1, 1, weights[3], 0))
    pl.when(tm < 15)(lambda: step(field3, field4, OWN_T + 1, 1, 1, weights[3], 0))
    pl.when(tm > 0)(lambda: step(field2, field3, -1, 1, 1, weights[2], 0))
    pl.when(tm < 15)(lambda: step(field2, field3, OWN_T, 1, 1, weights[2], 0))
    arrived(None, sum_z(0))
    total[z_next] = total[z_next] + total_in[0]
    start(None, sum_z(2))
    finish(0, 2, 3)
    sent()
    arrived(None, sum_z(1))
    arrived(None, sum_z(2))
    grad[...] = total[z] + total_in[1] + total_in[2]


def place(noise_in, grad_in, noise, grad, done):
    copies = [
        pltpu.make_async_copy(noise_in, noise, done.at[0]),
        pltpu.make_async_copy(grad_in, grad, done.at[1]),
    ]
    for one in copies:
        one.start()
    for one in copies:
        one.wait()


def vmem(*shape):
    return pltpu.VMEM(shape, jnp.float32)


def body(lats, cotangent, iterates, range_field):
    anywhere = pl.BlockSpec(memory_space=pltpu.HBM)
    inside = pl.BlockSpec(memory_space=pltpu.VMEM)
    count = 128
    return pl.pallas_call(
        functools.partial(kernel, lats, Sems()),
        out_shape=(
            jax.ShapeDtypeStruct(cotangent.shape, jnp.float32),
            jax.ShapeDtypeStruct(range_field.shape, jnp.float32),
        ),
        in_specs=[anywhere] * 3,
        out_specs=(inside, inside),
        scratch_shapes=[
            vmem(OWN_T, OWN, 2048),
            vmem(3, OWN_T, OWN, 2048),
            vmem(SLICES, ROWS * SEG, 128),
            vmem(SLICES, ROWS * SEG, 128),
            vmem(SLICES, ROWS * SEG, 128),
            vmem(OWN_T, OWN * SEG, 128),
            vmem(ROWS * SEG, 128),
            vmem(16, OWN, 128),
            vmem(2, PAD, 5 * SEG, 128),
            vmem(16, OWN, 128),
            vmem(3, 4, OWN, 128),
            vmem(4, OWN, 128),
            vmem(3, OWN, 128),
            pltpu.SemaphoreType.DMA((count,)),
            pltpu.SemaphoreType.DMA((count,)),
            pltpu.SemaphoreType.DMA((6,)),
        ],
        compiler_params=pltpu.CompilerParams(
            collective_id=0, has_side_effects=True, vmem_limit_bytes=60 << 20
        ),
        name="adjoint",
    )(cotangent, iterates, range_field)


def solution(mesh):
    placed = (P("tm", "lat", None), P(None, "tm", "lat", None), P("lat", "tm"))
    return jax.shard_map(
        functools.partial(body, mesh.shape["lat"]),
        mesh=mesh,
        in_specs=placed,
        out_specs=(P("tm", "lat", None), P("lat", "tm")),
        check_vma=False,
    )
```

```python
import functools
import math

import jax
import jax.numpy as jnp
from jax import lax
from jax.experimental import pallas as pl
from jax.experimental.pallas import tpu as pltpu
from jax.sharding import PartitionSpec as P

MESH = pl.DeviceIdType.MESH
SEG = 16
OWN = 16
PAD = 3
ROWS = OWN + 2 * PAD
OWN_T = 4
SLICES = OWN_T + 2 * PAD
SHARE = ((0, 5), (5, 4), (9, 4), (13, 3))


def step_weights():
    centre_value = 6.525
    spread_value = 6.475
    root_order = (3, 0, 2, 1)
    return [
        1.0 / (centre_value + spread_value * math.cos(math.pi * (2 * section + 1) / 8.0))
        for section in root_order
    ]


def at_row(row):
    return (row + PAD) * SEG


class Sems:
    def __init__(self):
        self.names = {}

    def __call__(self, *key):
        return self.names.setdefault(key, len(self.names))


def kernel(
    lats, sem_of, cot, its, rng, noise, grad,
    cin, xin, field4, field3, field2, rows_out, coef, gathered, edges, relay, part, part_in, total, total_in,
    send, recv, local,
):
    weights = step_weights()
    tm = lax.axis_index("tm")
    lat = lax.axis_index("lat")
    z, y = lax.div(tm, 4), lax.rem(tm, 4)
    z_next, z_prev, z_far = lax.rem(z + 1, 4), lax.rem(z + 3, 4), lax.rem(z + 2, 4)
    lat_next, lat_prev = lax.rem(lat + 1, lats), lax.rem(lat + lats - 1, lats)

    def dev(zz, yy, ll=None):
        return (zz * 4 + yy, lat if ll is None else ll)

    barrier = pltpu.get_barrier_semaphore()

    def greet(device):
        pl.semaphore_signal(barrier, inc=1, device_id=device, device_id_type=MESH)

    for other in (z_next, z_prev):
        greet(dev(other, y))

    @pl.when(y == 0)
    def _():
        for plane in (1, 2, 3):
            greet(dev(z_prev, plane))

    @pl.when(y == 3)
    def _():
        for plane in (0, 1, 2):
            greet(dev(z_next, plane))

    for other in range(4):
        greet(dev(z, lax.rem(y + other, 4), lat_next))
        greet(dev(z, lax.rem(y + other, 4), lat_prev))
        if other:
            greet(dev(z, lax.rem(y + other, 4)))

    loads = [pltpu.make_async_copy(cot.at[t], cin.at[t], local.at[t]) for t in range(OWN_T)]
    for t in (3, 0, 2, 1):
        loads[t].start()
    load_range = pltpu.make_async_copy(rng, gathered.at[y * 4 + z], local.at[4])
    load_range.start()
    load_its = pltpu.make_async_copy(its, xin, local.at[5])
    load_its.start()

    def zero(ref, t, row, rows):
        ref[t + PAD, pl.ds(at_row(row), rows * SEG), :] = jnp.zeros((rows * SEG, 128), jnp.float32)

    @pl.when(lat == 0)
    def _():
        for ref in (field4, field3, field2):
            for t in range(-PAD, OWN_T + PAD):
                zero(ref, t, -PAD, PAD)

    @pl.when(lat == lats - 1)
    def _():
        for ref in (field4, field3, field2):
            for t in range(-PAD, OWN_T + PAD):
                zero(ref, t, OWN, PAD)

    @pl.when(tm == 0)
    def _():
        for ref in (field4, field3, field2):
            for t in range(-PAD, 0):
                zero(ref, t, -PAD, ROWS)

    @pl.when(tm == 15)
    def _():
        for ref in (field4, field3, field2):
            for t in range(OWN_T, OWN_T + PAD):
                zero(ref, t, -PAD, ROWS)

    ends = jnp.logical_or(y == 0, y == 3)

    @pl.when(ends)
    def _():
        pl.semaphore_wait(barrier, 14)

    @pl.when(jnp.logical_not(ends))
    def _():
        pl.semaphore_wait(barrier, 15)

    sends = []

    def copy(key, src, dst, device):
        index = sem_of(*key)
        return pltpu.make_async_remote_copy(
            src_ref=src, dst_ref=dst, send_sem=send.at[index], recv_sem=recv.at[index],
            device_id=device, device_id_type=MESH,
        )

    def start(condition, *made):
        if condition is None:
            for one in made:
                one.start()
        else:

            @pl.when(condition)
            def _():
                for one in made:
                    one.start()

        sends.append((condition, made))

    def arrived(condition, *made):
        if condition is None:
            for one in made:
                one.wait_recv()
        else:

            @pl.when(condition)
            def _():
                for one in made:
                    one.wait_recv()

    def sent():
        for condition, made in sends:
            if condition is None:
                for one in made:
                    one.wait_send()
            else:

                @pl.when(condition)
                def _():
                    for one in made:
                        one.wait_send()

        sends.clear()

    def block(ref, t, row, rows):
        return ref.at[t + PAD, pl.ds(at_row(row), rows * SEG), :]

    has_lat_prev, has_lat_next = lat > 0, lat < lats - 1

    def range_z(way):
        return copy(("rz", way), rng, gathered.at[y * 4 + z], dev(z_next if way > 0 else z_prev, y))

    def range_z_second():
        slot = gathered.at[y * 4 + z_prev]
        return copy(("rz2",), slot, slot, dev(z_next, y))

    def range_y(number, other):
        slot = gathered.at[y * 4 + (z, z_prev, z_next, z_far)[number]]
        return copy(("ry", number, other), slot, slot, dev(z, lax.rem(y + other, 4)))

    def share_range(number):
        for other in (1, 2, 3):
            start(None, range_y(number, other))

    def range_edge(way, other):
        slots = pl.ds(y * 4, 4)
        return copy(
            ("re", way, other),
            gathered.at[slots, pl.ds(8 if way > 0 else 0, 8), :],
            edges.at[0 if way > 0 else 1, slots],
            dev(z, lax.rem(y + other, 4), lat_next if way > 0 else lat_prev),
        )

    def lat_halo(way):
        own = pl.ds(PAD, OWN_T)
        if way > 0:
            src, dst = OWN - PAD, -PAD
        else:
            src, dst = 0, OWN
        return copy(
            ("lat", way),
            field4.at[own, pl.ds(at_row(src), PAD * SEG), :],
            field4.at[own, pl.ds(at_row(dst), PAD * SEG), :],
            dev(z, y, lat_next if way > 0 else lat_prev),
        )

    def slices(way, depth):
        return (OWN_T - depth, -depth) if way > 0 else (depth - 1, OWN_T - 1 + depth)

    def beside(way, depth):
        src, dst = slices(way, depth)
        return copy(
            ("t", way, depth), block(field4, src, 0, OWN), block(field4, dst, 0, OWN), dev(z, y + way)
        )

    def across(way):
        return dev(z_next, 0) if way > 0 else dev(z_prev, 3)

    def to_relay(way, depth, plane):
        first, rows = SHARE[plane]
        src, _ = slices(way, depth)
        return copy(
            ("a", way, depth),
            block(field4, src, first, rows),
            relay.at[(way + 1) // 2, depth - 1, pl.ds(0, rows * SEG)],
            dev(z, plane if way > 0 else 3 - plane),
        )

    def to_relay_send(way, depth, plane):
        first, rows = SHARE[plane]
        src, _ = slices(way, depth)
        return pltpu.make_async_remote_copy(
            src_ref=block(field4, src, first, rows),
            dst_ref=relay.at[(way + 1) // 2, depth - 1, pl.ds(0, rows * SEG)],
            send_sem=send.at[sem_of("as", way, depth, plane)],
            recv_sem=recv.at[sem_of("a", way, depth)],
            device_id=dev(z, plane if way > 0 else 3 - plane),
            device_id_type=MESH,
        )

    def from_relay(way, depth, plane):
        first, rows = SHARE[plane]
        src, dst = slices(way, depth)
        source = (
            block(field4, src, first, rows)
            if plane == 3
            else relay.at[(way + 1) // 2, depth - 1, pl.ds(0, rows * SEG)]
        )
        return copy(("b", way, depth, plane), source, block(field4, dst, first, rows), across(way))

    corners = ((1, -2, 2), (1, OWN, 2), (2, -1, 1), (2, OWN, 1))

    def corner(way, number, crossing):
        depth, row, rows = corners[number]
        src, dst = slices(way, depth)
        return copy(
            ("c", way, number),
            block(field4, src, row, rows),
            block(field4, dst, row, rows),
            across(way) if crossing else dev(z, y + way),
        )

    def is_source(way):
        return jnp.logical_and(y == 3, z < 3) if way > 0 else jnp.logical_and(y == 0, z > 0)

    def is_target(way):
        return jnp.logical_and(y == 0, z > 0) if way > 0 else jnp.logical_and(y == 3, z < 3)

    def is_relay(way, plane):
        return (
            jnp.logical_and(y == plane, z < 3) if way > 0 else jnp.logical_and(y == 3 - plane, z > 0)
        )

    def beside_out(way):
        return y < 3 if way > 0 else y > 0

    def beside_in(way):
        return y > 0 if way > 0 else y < 3

    def lat_edge(row):
        return has_lat_prev if row < 0 else has_lat_next

    def send_slices(depth):
        for way in (1, -1):
            start(
                is_source(way),
                *[to_relay_send(way, depth, plane) for plane in (0, 1, 2)],
                from_relay(way, depth, 3),
            )
            start(beside_out(way), beside(way, depth))

    def forward(depth):
        for way in (1, -1):
            for plane in (0, 1, 2):

                @pl.when(is_relay(way, plane))
                def _():
                    to_relay(way, depth, plane).wait_recv()
                    from_relay(way, depth, plane).start()

                sends.append((is_relay(way, plane), (from_relay(way, depth, plane),)))

    def wait_slices(depth):
        for way in (1, -1):
            arrived(beside_in(way), beside(way, depth))
            arrived(is_target(way), *[from_relay(way, depth, plane) for plane in range(4)])

    def send_corners():
        for way in (1, -1):
            for pair in ((0, 2), (1, 3)):
                inside = lat_edge(corners[pair[0]][1])
                start(
                    jnp.logical_and(beside_out(way), inside),
                    *[corner(way, number, False) for number in pair],
                )
                start(
                    jnp.logical_and(is_source(way), inside),
                    *[corner(way, number, True) for number in pair],
                )

    def wait_corners(depth):
        for way in (1, -1):
            for number in range(4):
                if corners[number][0] == depth:
                    inside = lat_edge(corners[number][1])
                    coming = jnp.logical_or(beside_in(way), is_target(way))
                    arrived(jnp.logical_and(coming, inside), corner(way, number, False))

    lane = lax.broadcasted_iota(jnp.int32, (SEG, 128), 1)

    def row_of(src, t, base):
        return src[t, pl.ds(base, SEG), :]

    def neighbours(src, t, base):
        cells = row_of(src, t, base)
        around = (
            row_of(src, t, base - SEG)
            + row_of(src, t, base + SEG)
            + row_of(src, t - 1, base)
            + row_of(src, t + 1, base)
        )
        west = pltpu.roll(cells, 1, 1)
        west = jnp.where(lane == 0, pltpu.roll(west, 1, 0), west)
        east = pltpu.roll(cells, 127, 1)
        east = jnp.where(lane == 127, pltpu.roll(east, SEG - 1, 0), east)
        return around + (west + east)

    def joined(src, t, base, weight, summed):
        cells = row_of(src, t, base)
        return cells - weight * (coef[pl.ds(base, SEG), :] * cells - summed)

    def stepped(src, t, base, weight):
        return joined(src, t, base, weight, neighbours(src, t, base))

    UNROLL = 8

    def step(dst, src, t_first, t_count, t_stride, weight, outer, how=None):
        def stepped_by(src, t, base, weight):
            if how == "gather":
                return neighbours(src, t, base)
            if how == "join":
                return joined(src, t, base, weight, row_of(dst, t, base))
            return stepped(src, t, base, weight)

        pieces = OWN // UNROLL

        def piece(i, carry):
            t = t_first + PAD + lax.div(i, pieces) * t_stride
            base = pl.multiple_of(at_row(0) + lax.rem(i, pieces) * (UNROLL * SEG), SEG)
            for row in range(UNROLL):
                here = base + row * SEG
                dst[t, pl.ds(here, SEG), :] = stepped_by(src, t, here, weight)
            return carry

        lax.fori_loop(0, t_count * pieces, piece, 0)

        def beyond(first, rows):
            def one(i, carry):
                t = t_first + PAD + i * t_stride
                for row in range(first, first + rows):
                    dst[t, pl.ds(at_row(row), SEG), :] = stepped_by(src, t, at_row(row), weight)
                return carry

            lax.fori_loop(0, t_count, one, 0)

        if outer:
            pl.when(has_lat_prev)(lambda: beyond(-outer, outer))
            pl.when(has_lat_next)(lambda: beyond(OWN, outer))

    def products(terms, first):
        def column(j, carry):
            for group in range(2):
                value = None
                for ref, k, t in terms:
                    adj = ref[t + PAD, pl.ds(at_row(group * 8) + j, 8, stride=SEG), :]
                    x = xin[k - 1, t, group * 8 : group * 8 + 8, pl.ds(pl.multiple_of(j * 128, 128), 128)]
                    term = (-weights[k]) * (adj * x)
                    value = term if value is None else value + term
                slot = lax.rem(j, 4) * 4 + lax.div(j, 4)
                rows = slice(group * 8, group * 8 + 8)
                part[slot, rows, :] = value if first else part[slot, rows, :] + value
            return carry

        lax.fori_loop(0, 16, column, 0)

    start(None, range_z(1), range_z(-1))
    load_range.wait()
    share_range(0)

    for t in (3, 0, 2, 1):
        loads[t].wait()
        for group in range(2):
            for j in range(16):
                field4[t + PAD, pl.ds(at_row(group * 8) + j, 8, stride=SEG), :] = cin[
                    t, group * 8 : group * 8 + 8, j * 128 : j * 128 + 128
                ]
    start(has_lat_next, lat_halo(1))
    start(has_lat_prev, lat_halo(-1))
    send_slices(1)
    arrived(None, range_z(1))
    start(None, range_z_second())
    share_range(1)
    arrived(None, range_z(-1))
    share_range(2)
    forward(1)
    arrived(None, range_z_second())
    share_range(3)
    start(has_lat_next, *[range_edge(1, other) for other in range(4)])
    start(has_lat_prev, *[range_edge(-1, other) for other in range(4)])
    send_slices(2)
    arrived(has_lat_prev, lat_halo(1))
    arrived(has_lat_next, lat_halo(-1))
    send_corners()
    load_its.wait()
    products([(field4, 3, t) for t in range(OWN_T)], True)
    forward(2)
    send_slices(3)
    step(field3, field4, 1, 2, 1, weights[3], 2, "gather")
    for number in range(4):
        for other in (1, 2, 3):
            arrived(None, range_y(number, other))
    for j in range(16):
        slot = (j % 4) * 4 + j // 4
        for group in range(2):
            coef[pl.ds(at_row(group * 8) + j, 8, stride=SEG), :] = (
                gathered[slot, group * 8 : group * 8 + 8, :] + 6.0
            )
    wait_slices(1)
    wait_corners(1)
    step(field3, field4, 0, 2, 3, weights[3], 2, "gather")
    forward(3)

    def edge_rows(side, row, first):
        for j in range(16):
            slot = (j % 4) * 4 + j // 4
            for i in range(2):
                coef[pl.ds(at_row(row + i) + j, 1), :] = edges[side, slot, first + i : first + i + 1, :] + 6.0

    arrived(has_lat_prev, *[range_edge(1, other) for other in range(4)])
    arrived(has_lat_next, *[range_edge(-1, other) for other in range(4)])
    pl.when(has_lat_prev)(lambda: edge_rows(0, -2, 6))
    pl.when(has_lat_next)(lambda: edge_rows(1, OWN, 0))
    step(field3, field4, 0, 4, 1, weights[3], 2, "join")
    step(field2, field3, 1, 2, 1, weights[2], 1)
    products([(field3, 2, t) for t in range(OWN_T)] + [(field2, 1, 1), (field2, 1, 2)], False)
    wait_slices(2)
    wait_corners(2)
    pl.when(tm > 0)(lambda: step(field3, field4, -1, 1, 1, weights[3], 1))
    pl.when(tm < 15)(lambda: step(field3, field4, OWN_T, 1, 1, weights[3], 1))
    step(field2, field3, 0, 2, 3, weights[2], 1)
    products([(field2, 1, 0), (field2, 1, 3)], False)

    def sum_y(other):
        target = lax.rem(y + other, 4)
        return copy(("sy", other), part.at[pl.ds(target * 4, 4)], part_in.at[other - 1], dev(z, target))

    def sum_z(number):
        which = (z_far, z_prev, z_next)[number]
        return copy(("sz", number), total.at[which], total_in.at[number], dev(which, y))

    def finish(t_first, t_count, t_stride):
        pieces = OWN // UNROLL

        def piece(i, carry):
            t = t_first + PAD + lax.div(i, pieces) * t_stride
            base = pl.multiple_of(at_row(0) + lax.rem(i, pieces) * (UNROLL * SEG), SEG)
            for row in range(UNROLL):
                here = base + row * SEG
                last = stepped(field2, t, here, weights[1])
                rows_out[t - PAD, pl.ds(here - at_row(0), SEG), :] = (
                    weights[3] * row_of(field4, t, here)
                    + weights[2] * row_of(field3, t, here)
                    + weights[1] * row_of(field2, t, here)
                    + weights[0] * last
                )
            return carry

        lax.fori_loop(0, t_count * pieces, piece, 0)

        def columns(i, carry):
            t = t_first + lax.div(i, 16) * t_stride
            j = lax.rem(i, 16)
            for group in range(2):
                noise[t, group * 8 : group * 8 + 8, pl.ds(pl.multiple_of(j * 128, 128), 128)] = rows_out[
                    t, pl.ds(group * 8 * SEG + j, 8, stride=SEG), :
                ]
            return carry

        lax.fori_loop(0, t_count * 16, columns, 0)

    for other in (1, 2, 3):
        start(None, sum_y(other))
    finish(1, 2, 1)
    for other in (1, 2, 3):
        arrived(None, sum_y(other))
    for zz in range(4):
        total[zz] = part[y * 4 + zz] + part_in[0, zz] + part_in[1, zz] + part_in[2, zz]
    start(None, sum_z(0), sum_z(1), sum_z(2))
    wait_slices(3)
    pl.when(tm > 0)(lambda: step(field3, field4, -2, 1, 1, weights[3], 0))
    pl.when(tm < 15)(lambda: step(field3, field4, OWN_T + 1, 1, 1, weights[3], 0))
    pl.when(tm > 0)(lambda: step(field2, field3, -1, 1, 1, weights[2], 0))
    pl.when(tm < 15)(lambda: step(field2, field3, OWN_T, 1, 1, weights[2], 0))
    finish(0, 2, 3)
    sent()
    for number in range(3):
        arrived(None, sum_z(number))
    grad[...] = total[z] + total_in[0] + total_in[1] + total_in[2]


def vmem(*shape):
    return pltpu.VMEM(shape, jnp.float32)


def body(lats, cotangent, iterates, range_field):
    anywhere = pl.BlockSpec(memory_space=pltpu.HBM)
    inside = pl.BlockSpec(memory_space=pltpu.VMEM)
    count = 128
    return pl.pallas_call(
        functools.partial(kernel, lats, Sems()),
        out_shape=(
            vmem(*cotangent.shape),
            vmem(*range_field.shape),
        ),
        in_specs=[anywhere] * 3,
        out_specs=(inside, inside),
        scratch_shapes=[
            vmem(OWN_T, OWN, 2048),
            vmem(3, OWN_T, OWN, 2048),
            vmem(SLICES, ROWS * SEG, 128),
            vmem(SLICES, ROWS * SEG, 128),
            vmem(SLICES, ROWS * SEG, 128),
            vmem(OWN_T, OWN * SEG, 128),
            vmem(ROWS * SEG, 128),
            vmem(16, OWN, 128),
            vmem(2, 16, 8, 128),
            vmem(2, PAD, 5 * SEG, 128),
            vmem(16, OWN, 128),
            vmem(3, 4, OWN, 128),
            vmem(4, OWN, 128),
            vmem(3, OWN, 128),
            pltpu.SemaphoreType.DMA((count,)),
            pltpu.SemaphoreType.DMA((count,)),
            pltpu.SemaphoreType.DMA((6,)),
        ],
        compiler_params=pltpu.CompilerParams(
            collective_id=0, has_side_effects=True, vmem_limit_bytes=56 << 20
        ),
        name="adjoint",
    )(cotangent, iterates, range_field)


def solution(mesh):
    placed = (P("tm", "lat", None), P(None, "tm", "lat", None), P("lat", "tm"))
    return jax.shard_map(
        functools.partial(body, mesh.shape["lat"]),
        mesh=mesh,
        in_specs=placed,
        out_specs=(P("tm", "lat", None), P("lat", "tm")),
        check_vma=False,
    )
```

```python
import functools
import math

import jax
import jax.numpy as jnp
from jax import lax
from jax.experimental import pallas as pl
from jax.experimental.pallas import tpu as pltpu
from jax.sharding import PartitionSpec as P

MESH = pl.DeviceIdType.MESH
SEG = 16
OWN = 16
PAD = 3
ROWS = OWN + 2 * PAD
OWN_T = 4
SLICES = OWN_T + 2 * PAD
SHARE = ((0, 5), (5, 4), (9, 4), (13, 3))


def step_weights():
    centre_value = 6.525
    spread_value = 6.475
    root_order = (3, 0, 2, 1)
    return [
        1.0 / (centre_value + spread_value * math.cos(math.pi * (2 * section + 1) / 8.0))
        for section in root_order
    ]


def at_row(row):
    return (row + PAD) * SEG


class Sems:
    def __init__(self):
        self.names = {}

    def __call__(self, *key):
        return self.names.setdefault(key, len(self.names))


def kernel(
    lats, sem_of, cot, its, rng, noise, grad,
    cin, xin, field4, field3, field2, rows_out, xrows, summed, coef, gathered, edges, relay, part, part_in, total, total_in,
    send, recv, local,
):
    weights = step_weights()
    tm = lax.axis_index("tm")
    lat = lax.axis_index("lat")
    z, y = lax.div(tm, 4), lax.rem(tm, 4)
    z_next, z_prev, z_far = lax.rem(z + 1, 4), lax.rem(z + 3, 4), lax.rem(z + 2, 4)
    lat_next, lat_prev = lax.rem(lat + 1, lats), lax.rem(lat + lats - 1, lats)

    def dev(zz, yy, ll=None):
        return (zz * 4 + yy, lat if ll is None else ll)

    barrier = pltpu.get_barrier_semaphore()

    def greet(device):
        pl.semaphore_signal(barrier, inc=1, device_id=device, device_id_type=MESH)

    for other in (z_next, z_prev):
        greet(dev(other, y))

    @pl.when(y == 0)
    def _():
        for plane in (1, 2, 3):
            greet(dev(z_prev, plane))

    @pl.when(y == 3)
    def _():
        for plane in (0, 1, 2):
            greet(dev(z_next, plane))

    for other in range(4):
        greet(dev(z, lax.rem(y + other, 4), lat_next))
        greet(dev(z, lax.rem(y + other, 4), lat_prev))
        if other:
            greet(dev(z, lax.rem(y + other, 4)))

    loads = [pltpu.make_async_copy(cot.at[t], cin.at[t], local.at[t]) for t in range(OWN_T)]
    for t in (3, 0, 2, 1):
        loads[t].start()
    load_range = pltpu.make_async_copy(rng, gathered.at[y * 4 + z], local.at[4])
    load_range.start()
    load_its = pltpu.make_async_copy(its, xin, local.at[5])
    load_its.start()

    def zero(ref, t, row, rows):
        ref[t + PAD, pl.ds(at_row(row), rows * SEG), :] = jnp.zeros((rows * SEG, 128), jnp.float32)

    @pl.when(lat == 0)
    def _():
        for ref in (field4, field3, field2):
            for t in range(-PAD, OWN_T + PAD):
                zero(ref, t, -PAD, PAD)

    @pl.when(lat == lats - 1)
    def _():
        for ref in (field4, field3, field2):
            for t in range(-PAD, OWN_T + PAD):
                zero(ref, t, OWN, PAD)

    @pl.when(tm == 0)
    def _():
        for ref in (field4, field3, field2):
            for t in range(-PAD, 0):
                zero(ref, t, -PAD, ROWS)

    @pl.when(tm == 15)
    def _():
        for ref in (field4, field3, field2):
            for t in range(OWN_T, OWN_T + PAD):
                zero(ref, t, -PAD, ROWS)

    ends = jnp.logical_or(y == 0, y == 3)

    @pl.when(ends)
    def _():
        pl.semaphore_wait(barrier, 14)

    @pl.when(jnp.logical_not(ends))
    def _():
        pl.semaphore_wait(barrier, 15)

    sends = []

    def copy(key, src, dst, device):
        index = sem_of(*key)
        return pltpu.make_async_remote_copy(
            src_ref=src, dst_ref=dst, send_sem=send.at[index], recv_sem=recv.at[index],
            device_id=device, device_id_type=MESH,
        )

    def start(condition, *made):
        if condition is None:
            for one in made:
                one.start()
        else:

            @pl.when(condition)
            def _():
                for one in made:
                    one.start()

        sends.append((condition, made))

    def arrived(condition, *made):
        if condition is None:
            for one in made:
                one.wait_recv()
        else:

            @pl.when(condition)
            def _():
                for one in made:
                    one.wait_recv()

    def sent():
        for condition, made in sends:
            if condition is None:
                for one in made:
                    one.wait_send()
            else:

                @pl.when(condition)
                def _():
                    for one in made:
                        one.wait_send()

        sends.clear()

    def block(ref, t, row, rows):
        return ref.at[t + PAD, pl.ds(at_row(row), rows * SEG), :]

    has_lat_prev, has_lat_next = lat > 0, lat < lats - 1

    def range_z(way):
        return copy(("rz", way), rng, gathered.at[y * 4 + z], dev(z_next if way > 0 else z_prev, y))

    def range_z_second():
        slot = gathered.at[y * 4 + z_prev]
        return copy(("rz2",), slot, slot, dev(z_next, y))

    def range_y(number, other):
        slot = gathered.at[y * 4 + (z, z_prev, z_next, z_far)[number]]
        return copy(("ry", number, other), slot, slot, dev(z, lax.rem(y + other, 4)))

    def share_range(number):
        for other in (1, 2, 3):
            start(None, range_y(number, other))

    def range_edge(way, other):
        slots = pl.ds(y * 4, 4)
        return copy(
            ("re", way, other),
            gathered.at[slots, pl.ds(8 if way > 0 else 0, 8), :],
            edges.at[0 if way > 0 else 1, slots],
            dev(z, lax.rem(y + other, 4), lat_next if way > 0 else lat_prev),
        )

    def lat_halo(way):
        own = pl.ds(PAD, OWN_T)
        if way > 0:
            src, dst = OWN - PAD, -PAD
        else:
            src, dst = 0, OWN
        return copy(
            ("lat", way),
            field4.at[own, pl.ds(at_row(src), PAD * SEG), :],
            field4.at[own, pl.ds(at_row(dst), PAD * SEG), :],
            dev(z, y, lat_next if way > 0 else lat_prev),
        )

    def slices(way, depth):
        return (OWN_T - depth, -depth) if way > 0 else (depth - 1, OWN_T - 1 + depth)

    def beside(way, depth):
        src, dst = slices(way, depth)
        return copy(
            ("t", way, depth), block(field4, src, 0, OWN), block(field4, dst, 0, OWN), dev(z, y + way)
        )

    def across(way):
        return dev(z_next, 0) if way > 0 else dev(z_prev, 3)

    def to_relay(way, depth, plane):
        first, rows = SHARE[plane]
        src, _ = slices(way, depth)
        return copy(
            ("a", way, depth),
            block(field4, src, first, rows),
            relay.at[(way + 1) // 2, depth - 1, pl.ds(0, rows * SEG)],
            dev(z, plane if way > 0 else 3 - plane),
        )

    def to_relay_send(way, depth, plane):
        first, rows = SHARE[plane]
        src, _ = slices(way, depth)
        return pltpu.make_async_remote_copy(
            src_ref=block(field4, src, first, rows),
            dst_ref=relay.at[(way + 1) // 2, depth - 1, pl.ds(0, rows * SEG)],
            send_sem=send.at[sem_of("as", way, depth, plane)],
            recv_sem=recv.at[sem_of("a", way, depth)],
            device_id=dev(z, plane if way > 0 else 3 - plane),
            device_id_type=MESH,
        )

    def from_relay(way, depth, plane):
        first, rows = SHARE[plane]
        src, dst = slices(way, depth)
        source = (
            block(field4, src, first, rows)
            if plane == 3
            else relay.at[(way + 1) // 2, depth - 1, pl.ds(0, rows * SEG)]
        )
        return copy(("b", way, depth, plane), source, block(field4, dst, first, rows), across(way))

    corners = ((1, -2, 2), (1, OWN, 2), (2, -1, 1), (2, OWN, 1))

    def corner(way, number, crossing):
        depth, row, rows = corners[number]
        src, dst = slices(way, depth)
        return copy(
            ("c", way, number),
            block(field4, src, row, rows),
            block(field4, dst, row, rows),
            across(way) if crossing else dev(z, y + way),
        )

    def is_source(way):
        return jnp.logical_and(y == 3, z < 3) if way > 0 else jnp.logical_and(y == 0, z > 0)

    def is_target(way):
        return jnp.logical_and(y == 0, z > 0) if way > 0 else jnp.logical_and(y == 3, z < 3)

    def is_relay(way, plane):
        return (
            jnp.logical_and(y == plane, z < 3) if way > 0 else jnp.logical_and(y == 3 - plane, z > 0)
        )

    def beside_out(way):
        return y < 3 if way > 0 else y > 0

    def beside_in(way):
        return y > 0 if way > 0 else y < 3

    def lat_edge(row):
        return has_lat_prev if row < 0 else has_lat_next

    def send_slices(depth):
        for way in (1, -1):
            start(
                is_source(way),
                *[to_relay_send(way, depth, plane) for plane in (0, 1, 2)],
                from_relay(way, depth, 3),
            )
            start(beside_out(way), beside(way, depth))

    def forward(depth):
        for way in (1, -1):
            for plane in (0, 1, 2):

                @pl.when(is_relay(way, plane))
                def _():
                    to_relay(way, depth, plane).wait_recv()
                    from_relay(way, depth, plane).start()

                sends.append((is_relay(way, plane), (from_relay(way, depth, plane),)))

    def wait_slices(depth):
        for way in (1, -1):
            arrived(beside_in(way), beside(way, depth))
            arrived(is_target(way), *[from_relay(way, depth, plane) for plane in range(4)])

    def send_corners():
        for way in (1, -1):
            for pair in ((0, 2), (1, 3)):
                inside = lat_edge(corners[pair[0]][1])
                start(
                    jnp.logical_and(beside_out(way), inside),
                    *[corner(way, number, False) for number in pair],
                )
                start(
                    jnp.logical_and(is_source(way), inside),
                    *[corner(way, number, True) for number in pair],
                )

    def wait_corners(depth):
        for way in (1, -1):
            for number in range(4):
                if corners[number][0] == depth:
                    inside = lat_edge(corners[number][1])
                    coming = jnp.logical_or(beside_in(way), is_target(way))
                    arrived(jnp.logical_and(coming, inside), corner(way, number, False))

    lane = lax.broadcasted_iota(jnp.int32, (SEG, 128), 1)

    def row_of(src, t, base):
        return src[t, pl.ds(base, SEG), :]

    def neighbours(src, t, base):
        cells = row_of(src, t, base)
        around = (
            row_of(src, t, base - SEG)
            + row_of(src, t, base + SEG)
            + row_of(src, t - 1, base)
            + row_of(src, t + 1, base)
        )
        west = pltpu.roll(cells, 1, 1)
        west = jnp.where(lane == 0, pltpu.roll(west, 1, 0), west)
        east = pltpu.roll(cells, 127, 1)
        east = jnp.where(lane == 127, pltpu.roll(east, SEG - 1, 0), east)
        return around + (west + east)

    def joined(src, t, base, weight, summed):
        cells = row_of(src, t, base)
        return cells - weight * (coef[pl.ds(base, SEG), :] * cells - summed)

    def stepped(src, t, base, weight):
        return joined(src, t, base, weight, neighbours(src, t, base))

    UNROLL = 8

    def step(dst, src, t_first, t_count, t_stride, weight, outer, how=None, k=None):
        def stepped_by(src, t, base, weight):
            if how == "gather":
                return neighbours(src, t, base)
            if how == "join":
                return joined(src, t, base, weight, row_of(dst, t, base))
            return stepped(src, t, base, weight)

        pieces = OWN // UNROLL

        def piece(i, carry):
            t = t_first + PAD + lax.div(i, pieces) * t_stride
            base = pl.multiple_of(at_row(0) + lax.rem(i, pieces) * (UNROLL * SEG), SEG)
            for row in range(UNROLL):
                here = base + row * SEG
                value = stepped_by(src, t, here, weight)
                dst[t, pl.ds(here, SEG), :] = value
                if k is not None:
                    add_product(k, t - PAD, here - at_row(0), value)
            return carry

        lax.fori_loop(0, t_count * pieces, piece, 0)

        def beyond(first, rows):
            def one(i, carry):
                t = t_first + PAD + i * t_stride
                for row in range(first, first + rows):
                    dst[t, pl.ds(at_row(row), SEG), :] = stepped_by(src, t, at_row(row), weight)
                return carry

            lax.fori_loop(0, t_count, one, 0)

        if outer:
            pl.when(has_lat_prev)(lambda: beyond(-outer, outer))
            pl.when(has_lat_next)(lambda: beyond(OWN, outer))

    def add_product(k, t, row, value):
        rows = pl.ds(row, SEG)
        summed[rows, :] = summed[rows, :] - weights[k] * (value * xrows[(k - 1) * OWN_T + t, rows, :])

    def rows_of_x():
        def column(i, carry):
            k, j = lax.div(i, 16), lax.rem(i, 16)
            for t in range(OWN_T):
                for group in range(2):
                    xrows[k * OWN_T + t, pl.ds(group * 8 * SEG + j, 8, stride=SEG), :] = xin[
                        k, t, group * 8 : group * 8 + 8, pl.ds(pl.multiple_of(j * 128, 128), 128)
                    ]
            return carry

        lax.fori_loop(0, 48, column, 0)

    def first_products():
        def piece(i, carry):
            for row in range(UNROLL):
                here = pl.multiple_of((i * UNROLL + row) * SEG, SEG)
                value = None
                for t in range(OWN_T):
                    term = row_of(field4, t + PAD, here + at_row(0)) * xrows[2 * OWN_T + t, pl.ds(here, SEG), :]
                    value = term if value is None else value + term
                summed[pl.ds(here, SEG), :] = (-weights[3]) * value
            return carry

        lax.fori_loop(0, OWN // UNROLL, piece, 0)

    def products_out():
        for j in range(16):
            for group in range(2):
                part[(j % 4) * 4 + j // 4, group * 8 : group * 8 + 8, :] = summed[
                    pl.ds(group * 8 * SEG + j, 8, stride=SEG), :
                ]

    start(None, range_z(1), range_z(-1))
    load_range.wait()
    share_range(0)

    for t in (3, 0, 2, 1):
        loads[t].wait()
        for group in range(2):
            for j in range(16):
                field4[t + PAD, pl.ds(at_row(group * 8) + j, 8, stride=SEG), :] = cin[
                    t, group * 8 : group * 8 + 8, j * 128 : j * 128 + 128
                ]
    start(has_lat_next, lat_halo(1))
    start(has_lat_prev, lat_halo(-1))
    send_slices(1)
    send_slices(2)
    arrived(None, range_z(1))
    start(None, range_z_second())
    share_range(1)
    arrived(None, range_z(-1))
    share_range(2)
    forward(1)
    arrived(None, range_z_second())
    share_range(3)
    start(has_lat_next, *[range_edge(1, other) for other in range(4)])
    start(has_lat_prev, *[range_edge(-1, other) for other in range(4)])
    arrived(has_lat_prev, lat_halo(1))
    arrived(has_lat_next, lat_halo(-1))
    send_corners()
    forward(2)
    send_slices(3)
    load_its.wait()
    rows_of_x()
    first_products()
    step(field3, field4, 1, 2, 1, weights[3], 2, "gather")
    for number in range(4):
        for other in (1, 2, 3):
            arrived(None, range_y(number, other))
    for j in range(16):
        slot = (j % 4) * 4 + j // 4
        for group in range(2):
            coef[pl.ds(at_row(group * 8) + j, 8, stride=SEG), :] = (
                gathered[slot, group * 8 : group * 8 + 8, :] + 6.0
            )
    wait_slices(1)
    wait_corners(1)
    step(field3, field4, 0, 2, 3, weights[3], 2, "gather")
    forward(3)

    def edge_rows(side, row, first):
        for j in range(16):
            slot = (j % 4) * 4 + j // 4
            for i in range(2):
                coef[pl.ds(at_row(row + i) + j, 1), :] = edges[side, slot, first + i : first + i + 1, :] + 6.0

    arrived(has_lat_prev, *[range_edge(1, other) for other in range(4)])
    arrived(has_lat_next, *[range_edge(-1, other) for other in range(4)])
    pl.when(has_lat_prev)(lambda: edge_rows(0, -2, 6))
    pl.when(has_lat_next)(lambda: edge_rows(1, OWN, 0))
    step(field3, field4, 0, 4, 1, weights[3], 2, "join", k=2)
    step(field2, field3, 1, 2, 1, weights[2], 1, k=1)
    wait_slices(2)
    wait_corners(2)
    pl.when(tm > 0)(lambda: step(field3, field4, -1, 1, 1, weights[3], 1))
    pl.when(tm < 15)(lambda: step(field3, field4, OWN_T, 1, 1, weights[3], 1))
    step(field2, field3, 0, 2, 3, weights[2], 1, k=1)
    products_out()

    def sum_y(other):
        target = lax.rem(y + other, 4)
        return copy(("sy", other), part.at[pl.ds(target * 4, 4)], part_in.at[other - 1], dev(z, target))

    def sum_z(number):
        which = (z_far, z_prev, z_next)[number]
        return copy(("sz", number), total.at[which], total_in.at[number], dev(which, y))

    def finish(t_first, t_count, t_stride):
        pieces = OWN // UNROLL

        def piece(i, carry):
            t = t_first + PAD + lax.div(i, pieces) * t_stride
            base = pl.multiple_of(at_row(0) + lax.rem(i, pieces) * (UNROLL * SEG), SEG)
            for row in range(UNROLL):
                here = base + row * SEG
                last = stepped(field2, t, here, weights[1])
                rows_out[t - PAD, pl.ds(here - at_row(0), SEG), :] = (
                    weights[3] * row_of(field4, t, here)
                    + weights[2] * row_of(field3, t, here)
                    + weights[1] * row_of(field2, t, here)
                    + weights[0] * last
                )
            return carry

        lax.fori_loop(0, t_count * pieces, piece, 0)

        def columns(i, carry):
            t = t_first + lax.div(i, 16) * t_stride
            j = lax.rem(i, 16)
            for group in range(2):
                noise[t, group * 8 : group * 8 + 8, pl.ds(pl.multiple_of(j * 128, 128), 128)] = rows_out[
                    t, pl.ds(group * 8 * SEG + j, 8, stride=SEG), :
                ]
            return carry

        lax.fori_loop(0, t_count * 16, columns, 0)

    for other in (1, 2, 3):
        start(None, sum_y(other))
    finish(1, 2, 1)
    for other in (1, 2, 3):
        arrived(None, sum_y(other))
    for zz in range(4):
        total[zz] = part[y * 4 + zz] + part_in[0, zz] + part_in[1, zz] + part_in[2, zz]
    start(None, sum_z(0), sum_z(1), sum_z(2))
    wait_slices(3)
    pl.when(tm > 0)(lambda: step(field3, field4, -2, 1, 1, weights[3], 0))
    pl.when(tm < 15)(lambda: step(field3, field4, OWN_T + 1, 1, 1, weights[3], 0))
    pl.when(tm > 0)(lambda: step(field2, field3, -1, 1, 1, weights[2], 0))
    pl.when(tm < 15)(lambda: step(field2, field3, OWN_T, 1, 1, weights[2], 0))
    finish(0, 2, 3)
    sent()
    for number in range(3):
        arrived(None, sum_z(number))
    grad[...] = total[z] + total_in[0] + total_in[1] + total_in[2]


def vmem(*shape):
    return pltpu.VMEM(shape, jnp.float32)


def body(lats, cotangent, iterates, range_field):
    anywhere = pl.BlockSpec(memory_space=pltpu.HBM)
    inside = pl.BlockSpec(memory_space=pltpu.VMEM)
    count = 128
    return pl.pallas_call(
        functools.partial(kernel, lats, Sems()),
        out_shape=(
            vmem(*cotangent.shape),
            vmem(*range_field.shape),
        ),
        in_specs=[anywhere] * 3,
        out_specs=(inside, inside),
        scratch_shapes=[
            vmem(OWN_T, OWN, 2048),
            vmem(3, OWN_T, OWN, 2048),
            vmem(SLICES, ROWS * SEG, 128),
            vmem(SLICES, ROWS * SEG, 128),
            vmem(SLICES, ROWS * SEG, 128),
            vmem(OWN_T, OWN * SEG, 128),
            vmem(3 * OWN_T, OWN * SEG, 128),
            vmem(OWN * SEG, 128),
            vmem(ROWS * SEG, 128),
            vmem(16, OWN, 128),
            vmem(2, 16, 8, 128),
            vmem(2, PAD, 5 * SEG, 128),
            vmem(16, OWN, 128),
            vmem(3, 4, OWN, 128),
            vmem(4, OWN, 128),
            vmem(3, OWN, 128),
            pltpu.SemaphoreType.DMA((count,)),
            pltpu.SemaphoreType.DMA((count,)),
            pltpu.SemaphoreType.DMA((6,)),
        ],
        compiler_params=pltpu.CompilerParams(
            collective_id=0, has_side_effects=True, vmem_limit_bytes=56 << 20
        ),
        name="adjoint",
    )(cotangent, iterates, range_field)


def solution(mesh):
    placed = (P("tm", "lat", None), P(None, "tm", "lat", None), P("lat", "tm"))
    return jax.shard_map(
        functools.partial(body, mesh.shape["lat"]),
        mesh=mesh,
        in_specs=placed,
        out_specs=(P("tm", "lat", None), P("lat", "tm")),
        check_vma=False,
    )
```

```python
import functools
import math

import jax
import jax.numpy as jnp
from jax import lax
from jax.experimental import pallas as pl
from jax.experimental.pallas import tpu as pltpu
from jax.sharding import PartitionSpec as P

MESH = pl.DeviceIdType.MESH
SEG = 16
OWN = 16
PAD = 3
ROWS = OWN + 2 * PAD
OWN_T = 4
SLICES = OWN_T + 2 * PAD
SHARE = ((0, 5), (5, 4), (9, 4), (13, 3))


def step_weights():
    centre_value = 6.525
    spread_value = 6.475
    root_order = (3, 0, 2, 1)
    return [
        1.0 / (centre_value + spread_value * math.cos(math.pi * (2 * section + 1) / 8.0))
        for section in root_order
    ]


def at_row(row):
    return (row + PAD) * SEG


class Sems:
    def __init__(self):
        self.names = {}

    def __call__(self, *key):
        return self.names.setdefault(key, len(self.names))


def kernel(
    lats, sem_of, cot, its, rng, noise, grad,
    cin, xin, field4, field3, field2, rows_out, xrows, summed, coef, gathered, edges, relay, part, part_in, total, total_in,
    send, recv, local,
):
    weights = step_weights()
    tm = lax.axis_index("tm")
    lat = lax.axis_index("lat")
    z, y = lax.div(tm, 4), lax.rem(tm, 4)
    z_next, z_prev, z_far = lax.rem(z + 1, 4), lax.rem(z + 3, 4), lax.rem(z + 2, 4)
    lat_next, lat_prev = lax.rem(lat + 1, lats), lax.rem(lat + lats - 1, lats)

    def dev(zz, yy, ll=None):
        return (zz * 4 + yy, lat if ll is None else ll)

    barrier = pltpu.get_barrier_semaphore()

    def greet(device):
        pl.semaphore_signal(barrier, inc=1, device_id=device, device_id_type=MESH)

    for other in (z_next, z_prev):
        greet(dev(other, y))

    @pl.when(y == 0)
    def _():
        for plane in (1, 2, 3):
            greet(dev(z_prev, plane))

    @pl.when(y == 3)
    def _():
        for plane in (0, 1, 2):
            greet(dev(z_next, plane))

    for other in range(4):
        greet(dev(z, lax.rem(y + other, 4), lat_next))
        greet(dev(z, lax.rem(y + other, 4), lat_prev))
        if other:
            greet(dev(z, lax.rem(y + other, 4)))

    loads = [pltpu.make_async_copy(cot.at[t], cin.at[t], local.at[t]) for t in range(OWN_T)]
    for t in (3, 0, 2, 1):
        loads[t].start()
    load_range = pltpu.make_async_copy(rng, gathered.at[y * 4 + z], local.at[4])
    load_range.start()
    load_its = pltpu.make_async_copy(its, xin, local.at[5])
    load_its.start()

    def zero(ref, t, row, rows):
        ref[t + PAD, pl.ds(at_row(row), rows * SEG), :] = jnp.zeros((rows * SEG, 128), jnp.float32)

    @pl.when(lat == 0)
    def _():
        for ref in (field4, field3, field2):
            for t in range(-PAD, OWN_T + PAD):
                zero(ref, t, -PAD, PAD)

    @pl.when(lat == lats - 1)
    def _():
        for ref in (field4, field3, field2):
            for t in range(-PAD, OWN_T + PAD):
                zero(ref, t, OWN, PAD)

    @pl.when(tm == 0)
    def _():
        for ref in (field4, field3, field2):
            for t in range(-PAD, 0):
                zero(ref, t, -PAD, ROWS)

    @pl.when(tm == 15)
    def _():
        for ref in (field4, field3, field2):
            for t in range(OWN_T, OWN_T + PAD):
                zero(ref, t, -PAD, ROWS)

    ends = jnp.logical_or(y == 0, y == 3)

    @pl.when(ends)
    def _():
        pl.semaphore_wait(barrier, 14)

    @pl.when(jnp.logical_not(ends))
    def _():
        pl.semaphore_wait(barrier, 15)

    sends = []

    def copy(key, src, dst, device):
        index = sem_of(*key)
        return pltpu.make_async_remote_copy(
            src_ref=src, dst_ref=dst, send_sem=send.at[index], recv_sem=recv.at[index],
            device_id=device, device_id_type=MESH,
        )

    def start(condition, *made):
        if condition is None:
            for one in made:
                one.start()
        else:

            @pl.when(condition)
            def _():
                for one in made:
                    one.start()

        sends.append((condition, made))

    def arrived(condition, *made):
        if condition is None:
            for one in made:
                one.wait_recv()
        else:

            @pl.when(condition)
            def _():
                for one in made:
                    one.wait_recv()

    def sent():
        for condition, made in sends:
            if condition is None:
                for one in made:
                    one.wait_send()
            else:

                @pl.when(condition)
                def _():
                    for one in made:
                        one.wait_send()

        sends.clear()

    def block(ref, t, row, rows):
        return ref.at[t + PAD, pl.ds(at_row(row), rows * SEG), :]

    has_lat_prev, has_lat_next = lat > 0, lat < lats - 1

    def range_z(way):
        return copy(("rz", way), rng, gathered.at[y * 4 + z], dev(z_next if way > 0 else z_prev, y))

    def range_z_second():
        slot = gathered.at[y * 4 + z_prev]
        return copy(("rz2",), slot, slot, dev(z_next, y))

    def range_y(number, other):
        slot = gathered.at[y * 4 + (z, z_prev, z_next, z_far)[number]]
        return copy(("ry", number, other), slot, slot, dev(z, lax.rem(y + other, 4)))

    def share_range(number):
        for other in (1, 2, 3):
            start(None, range_y(number, other))

    def range_edge(way, other):
        slots = pl.ds(y * 4, 4)
        return copy(
            ("re", way, other),
            gathered.at[slots, pl.ds(8 if way > 0 else 0, 8), :],
            edges.at[0 if way > 0 else 1, slots],
            dev(z, lax.rem(y + other, 4), lat_next if way > 0 else lat_prev),
        )

    def lat_halo(way):
        own = pl.ds(PAD, OWN_T)
        if way > 0:
            src, dst = OWN - PAD, -PAD
        else:
            src, dst = 0, OWN
        return copy(
            ("lat", way),
            field4.at[own, pl.ds(at_row(src), PAD * SEG), :],
            field4.at[own, pl.ds(at_row(dst), PAD * SEG), :],
            dev(z, y, lat_next if way > 0 else lat_prev),
        )

    def slices(way, depth):
        return (OWN_T - depth, -depth) if way > 0 else (depth - 1, OWN_T - 1 + depth)

    def beside(way, depth):
        src, dst = slices(way, depth)
        return copy(
            ("t", way, depth), block(field4, src, 0, OWN), block(field4, dst, 0, OWN), dev(z, y + way)
        )

    def across(way):
        return dev(z_next, 0) if way > 0 else dev(z_prev, 3)

    def to_relay(way, depth, plane):
        first, rows = SHARE[plane]
        src, _ = slices(way, depth)
        return copy(
            ("a", way, depth),
            block(field4, src, first, rows),
            relay.at[(way + 1) // 2, depth - 1, pl.ds(0, rows * SEG)],
            dev(z, plane if way > 0 else 3 - plane),
        )

    def to_relay_send(way, depth, plane):
        first, rows = SHARE[plane]
        src, _ = slices(way, depth)
        return pltpu.make_async_remote_copy(
            src_ref=block(field4, src, first, rows),
            dst_ref=relay.at[(way + 1) // 2, depth - 1, pl.ds(0, rows * SEG)],
            send_sem=send.at[sem_of("as", way, depth, plane)],
            recv_sem=recv.at[sem_of("a", way, depth)],
            device_id=dev(z, plane if way > 0 else 3 - plane),
            device_id_type=MESH,
        )

    def from_relay(way, depth, plane):
        first, rows = SHARE[plane]
        src, dst = slices(way, depth)
        source = (
            block(field4, src, first, rows)
            if plane == 3
            else relay.at[(way + 1) // 2, depth - 1, pl.ds(0, rows * SEG)]
        )
        return copy(("b", way, depth, plane), source, block(field4, dst, first, rows), across(way))

    corners = ((1, -2, 2), (1, OWN, 2), (2, -1, 1), (2, OWN, 1))

    def corner(way, number, crossing):
        depth, row, rows = corners[number]
        src, dst = slices(way, depth)
        return copy(
            ("c", way, number),
            block(field4, src, row, rows),
            block(field4, dst, row, rows),
            across(way) if crossing else dev(z, y + way),
        )

    def is_source(way):
        return jnp.logical_and(y == 3, z < 3) if way > 0 else jnp.logical_and(y == 0, z > 0)

    def is_target(way):
        return jnp.logical_and(y == 0, z > 0) if way > 0 else jnp.logical_and(y == 3, z < 3)

    def is_relay(way, plane):
        return (
            jnp.logical_and(y == plane, z < 3) if way > 0 else jnp.logical_and(y == 3 - plane, z > 0)
        )

    def beside_out(way):
        return y < 3 if way > 0 else y > 0

    def beside_in(way):
        return y > 0 if way > 0 else y < 3

    def lat_edge(row):
        return has_lat_prev if row < 0 else has_lat_next

    def send_slices(depth):
        for way in (1, -1):
            start(
                is_source(way),
                *[to_relay_send(way, depth, plane) for plane in (0, 1, 2)],
                from_relay(way, depth, 3),
            )
            start(beside_out(way), beside(way, depth))

    def forward(depth):
        for way in (1, -1):
            for plane in (0, 1, 2):

                @pl.when(is_relay(way, plane))
                def _():
                    to_relay(way, depth, plane).wait_recv()
                    from_relay(way, depth, plane).start()

                sends.append((is_relay(way, plane), (from_relay(way, depth, plane),)))

    def wait_slices(depth):
        for way in (1, -1):
            arrived(beside_in(way), beside(way, depth))
            arrived(is_target(way), *[from_relay(way, depth, plane) for plane in range(4)])

    def send_corners():
        for way in (1, -1):
            for pair in ((0, 2), (1, 3)):
                inside = lat_edge(corners[pair[0]][1])
                start(
                    jnp.logical_and(beside_out(way), inside),
                    *[corner(way, number, False) for number in pair],
                )
                start(
                    jnp.logical_and(is_source(way), inside),
                    *[corner(way, number, True) for number in pair],
                )

    def wait_corners(depth):
        for way in (1, -1):
            for number in range(4):
                if corners[number][0] == depth:
                    inside = lat_edge(corners[number][1])
                    coming = jnp.logical_or(beside_in(way), is_target(way))
                    arrived(jnp.logical_and(coming, inside), corner(way, number, False))

    lane = lax.broadcasted_iota(jnp.int32, (SEG, 128), 1)

    def row_of(src, t, base):
        return src[t, pl.ds(base, SEG), :]

    def neighbours(src, t, base):
        cells = row_of(src, t, base)
        around = (
            row_of(src, t, base - SEG)
            + row_of(src, t, base + SEG)
            + row_of(src, t - 1, base)
            + row_of(src, t + 1, base)
        )
        west = pltpu.roll(cells, 1, 1)
        west = jnp.where(lane == 0, pltpu.roll(west, 1, 0), west)
        east = pltpu.roll(cells, 127, 1)
        east = jnp.where(lane == 127, pltpu.roll(east, SEG - 1, 0), east)
        return around + (west + east)

    def joined(src, t, base, weight, summed):
        cells = row_of(src, t, base)
        return cells - weight * (coef[pl.ds(base, SEG), :] * cells - summed)

    def stepped(src, t, base, weight):
        return joined(src, t, base, weight, neighbours(src, t, base))

    UNROLL = 8

    def step(dst, src, t_first, t_count, t_stride, weight, outer, how=None, k=None):
        def stepped_by(src, t, base, weight):
            if how == "gather":
                return neighbours(src, t, base)
            if how == "join":
                return joined(src, t, base, weight, row_of(dst, t, base))
            return stepped(src, t, base, weight)

        pieces = OWN // UNROLL

        def piece(i, carry):
            t = t_first + PAD + lax.div(i, pieces) * t_stride
            base = pl.multiple_of(at_row(0) + lax.rem(i, pieces) * (UNROLL * SEG), SEG)
            for row in range(UNROLL):
                here = base + row * SEG
                value = stepped_by(src, t, here, weight)
                dst[t, pl.ds(here, SEG), :] = value
                if k is not None:
                    add_product(k, t - PAD, here - at_row(0), value)
            return carry

        lax.fori_loop(0, t_count * pieces, piece, 0)

        def beyond(first, rows):
            def one(i, carry):
                t = t_first + PAD + i * t_stride
                for row in range(first, first + rows):
                    dst[t, pl.ds(at_row(row), SEG), :] = stepped_by(src, t, at_row(row), weight)
                return carry

            lax.fori_loop(0, t_count, one, 0)

        if outer:
            pl.when(has_lat_prev)(lambda: beyond(-outer, outer))
            pl.when(has_lat_next)(lambda: beyond(OWN, outer))

    def add_product(k, t, row, value):
        rows = pl.ds(row, SEG)
        summed[rows, :] = summed[rows, :] - weights[k] * (value * xrows[(k - 1) * OWN_T + t, rows, :])

    def rows_of_x():
        def column(i, carry):
            k, j = lax.div(i, 16), lax.rem(i, 16)
            for t in range(OWN_T):
                for group in range(2):
                    xrows[k * OWN_T + t, pl.ds(group * 8 * SEG + j, 8, stride=SEG), :] = xin[
                        k, t, group * 8 : group * 8 + 8, pl.ds(pl.multiple_of(j * 128, 128), 128)
                    ]
            return carry

        lax.fori_loop(0, 48, column, 0)

    def first_products():
        def piece(i, carry):
            for row in range(UNROLL):
                here = pl.multiple_of((i * UNROLL + row) * SEG, SEG)
                value = None
                for t in range(OWN_T):
                    term = row_of(field4, t + PAD, here + at_row(0)) * xrows[2 * OWN_T + t, pl.ds(here, SEG), :]
                    value = term if value is None else value + term
                summed[pl.ds(here, SEG), :] = (-weights[3]) * value
            return carry

        lax.fori_loop(0, OWN // UNROLL, piece, 0)

    def products_out():
        for j in range(16):
            for group in range(2):
                part[(j % 4) * 4 + j // 4, group * 8 : group * 8 + 8, :] = summed[
                    pl.ds(group * 8 * SEG + j, 8, stride=SEG), :
                ]

    start(None, range_z(1), range_z(-1))
    load_range.wait()
    share_range(0)

    for t in (3, 0, 2, 1):
        loads[t].wait()
        for group in range(2):
            for j in range(16):
                field4[t + PAD, pl.ds(at_row(group * 8) + j, 8, stride=SEG), :] = cin[
                    t, group * 8 : group * 8 + 8, j * 128 : j * 128 + 128
                ]
    start(has_lat_next, lat_halo(1))
    start(has_lat_prev, lat_halo(-1))
    send_slices(1)
    send_slices(2)
    arrived(None, range_z(1))
    start(None, range_z_second())
    share_range(1)
    arrived(None, range_z(-1))
    share_range(2)
    forward(1)
    arrived(has_lat_prev, lat_halo(1))
    arrived(has_lat_next, lat_halo(-1))
    send_corners()
    forward(2)
    arrived(None, range_z_second())
    share_range(3)
    start(has_lat_next, *[range_edge(1, other) for other in range(4)])
    start(has_lat_prev, *[range_edge(-1, other) for other in range(4)])
    send_slices(3)
    load_its.wait()
    rows_of_x()
    first_products()
    step(field3, field4, 1, 2, 1, weights[3], 2, "gather")
    for number in range(4):
        for other in (1, 2, 3):
            arrived(None, range_y(number, other))
    for j in range(16):
        slot = (j % 4) * 4 + j // 4
        for group in range(2):
            coef[pl.ds(at_row(group * 8) + j, 8, stride=SEG), :] = (
                gathered[slot, group * 8 : group * 8 + 8, :] + 6.0
            )
    wait_slices(1)
    wait_corners(1)
    step(field3, field4, 0, 2, 3, weights[3], 2, "gather")
    forward(3)

    def edge_rows(side, row, first):
        for j in range(16):
            slot = (j % 4) * 4 + j // 4
            for i in range(2):
                coef[pl.ds(at_row(row + i) + j, 1), :] = edges[side, slot, first + i : first + i + 1, :] + 6.0

    arrived(has_lat_prev, *[range_edge(1, other) for other in range(4)])
    arrived(has_lat_next, *[range_edge(-1, other) for other in range(4)])
    pl.when(has_lat_prev)(lambda: edge_rows(0, -2, 6))
    pl.when(has_lat_next)(lambda: edge_rows(1, OWN, 0))
    step(field3, field4, 0, 4, 1, weights[3], 2, "join", k=2)
    step(field2, field3, 1, 2, 1, weights[2], 1, k=1)
    wait_slices(2)
    wait_corners(2)
    pl.when(tm > 0)(lambda: step(field3, field4, -1, 1, 1, weights[3], 1))
    pl.when(tm < 15)(lambda: step(field3, field4, OWN_T, 1, 1, weights[3], 1))
    step(field2, field3, 0, 2, 3, weights[2], 1, k=1)
    products_out()

    def sum_y(other):
        target = lax.rem(y + other, 4)
        return copy(("sy", other), part.at[pl.ds(target * 4, 4)], part_in.at[other - 1], dev(z, target))

    def sum_z(number):
        which = (z_far, z_prev, z_next)[number]
        return copy(("sz", number), total.at[which], total_in.at[number], dev(which, y))

    def finish(t_first, t_count, t_stride):
        pieces = OWN // UNROLL

        def piece(i, carry):
            t = t_first + PAD + lax.div(i, pieces) * t_stride
            base = pl.multiple_of(at_row(0) + lax.rem(i, pieces) * (UNROLL * SEG), SEG)
            for row in range(UNROLL):
                here = base + row * SEG
                last = stepped(field2, t, here, weights[1])
                rows_out[t - PAD, pl.ds(here - at_row(0), SEG), :] = (
                    weights[3] * row_of(field4, t, here)
                    + weights[2] * row_of(field3, t, here)
                    + weights[1] * row_of(field2, t, here)
                    + weights[0] * last
                )
            return carry

        lax.fori_loop(0, t_count * pieces, piece, 0)

        def columns(i, carry):
            t = t_first + lax.div(i, 16) * t_stride
            j = lax.rem(i, 16)
            for group in range(2):
                noise[t, group * 8 : group * 8 + 8, pl.ds(pl.multiple_of(j * 128, 128), 128)] = rows_out[
                    t, pl.ds(group * 8 * SEG + j, 8, stride=SEG), :
                ]
            return carry

        lax.fori_loop(0, t_count * 16, columns, 0)

    for other in (1, 2, 3):
        start(None, sum_y(other))
    finish(1, 2, 1)
    for other in (1, 2, 3):
        arrived(None, sum_y(other))
    for zz in range(4):
        total[zz] = part[y * 4 + zz] + part_in[0, zz] + part_in[1, zz] + part_in[2, zz]
    start(None, sum_z(0), sum_z(1), sum_z(2))
    wait_slices(3)
    pl.when(tm > 0)(lambda: step(field3, field4, -2, 1, 1, weights[3], 0))
    pl.when(tm < 15)(lambda: step(field3, field4, OWN_T + 1, 1, 1, weights[3], 0))
    pl.when(tm > 0)(lambda: step(field2, field3, -1, 1, 1, weights[2], 0))
    pl.when(tm < 15)(lambda: step(field2, field3, OWN_T, 1, 1, weights[2], 0))
    finish(0, 2, 3)
    sent()
    for number in range(3):
        arrived(None, sum_z(number))
    grad[...] = total[z] + total_in[0] + total_in[1] + total_in[2]


def vmem(*shape):
    return pltpu.VMEM(shape, jnp.float32)


def body(lats, cotangent, iterates, range_field):
    anywhere = pl.BlockSpec(memory_space=pltpu.HBM)
    inside = pl.BlockSpec(memory_space=pltpu.VMEM)
    count = 128
    return pl.pallas_call(
        functools.partial(kernel, lats, Sems()),
        out_shape=(
            vmem(*cotangent.shape),
            vmem(*range_field.shape),
        ),
        in_specs=[anywhere] * 3,
        out_specs=(inside, inside),
        scratch_shapes=[
            vmem(OWN_T, OWN, 2048),
            vmem(3, OWN_T, OWN, 2048),
            vmem(SLICES, ROWS * SEG, 128),
            vmem(SLICES, ROWS * SEG, 128),
            vmem(SLICES, ROWS * SEG, 128),
            vmem(OWN_T, OWN * SEG, 128),
            vmem(3 * OWN_T, OWN * SEG, 128),
            vmem(OWN * SEG, 128),
            vmem(ROWS * SEG, 128),
            vmem(16, OWN, 128),
            vmem(2, 16, 8, 128),
            vmem(2, PAD, 5 * SEG, 128),
            vmem(16, OWN, 128),
            vmem(3, 4, OWN, 128),
            vmem(4, OWN, 128),
            vmem(3, OWN, 128),
            pltpu.SemaphoreType.DMA((count,)),
            pltpu.SemaphoreType.DMA((count,)),
            pltpu.SemaphoreType.DMA((6,)),
        ],
        compiler_params=pltpu.CompilerParams(
            collective_id=0, has_side_effects=True, vmem_limit_bytes=56 << 20
        ),
        name="adjoint",
    )(cotangent, iterates, range_field)


def solution(mesh):
    placed = (P("tm", "lat", None), P(None, "tm", "lat", None), P("lat", "tm"))
    return jax.shard_map(
        functools.partial(body, mesh.shape["lat"]),
        mesh=mesh,
        in_specs=placed,
        out_specs=(P("tm", "lat", None), P("lat", "tm")),
        check_vma=False,
    )
```
